32 devices in a mesh: groups: 2 (over x), seq: 16 (over z, y, core).
Axes of the slice: x: 2, y: 2, z: 4, core: 2. Of those that a mesh axis runs over, the one named last changes fastest.
Arguments:
- atoms: bfloat16 [2, 8192, 128], P('groups', 'seq'), parts along dimension 0, may hold values from -6 to 6
- s_cond: bfloat16 [2048, 768], P(('groups', 'seq')), parts along dimension 0, may hold values from -6 to 6
- token_start: int32 [2048], P(('groups', 'seq')), parts along dimension 0, may hold values from 0 to 8191, as said below
- token_len: int32 [2048], P(('groups', 'seq')), parts along dimension 0, may hold values from 1 to 12, as said below
- atom_mask: int32 [16384], P(('groups', 'seq')), parts along dimension 0, may hold values 0 or 1
- atom_bias: float32 [8, 8192, 128], P('groups', 'seq'), parts along dimension 0, may hold values from -4 to 250
- pair_bias: bfloat16 [32, 1024, 1024], P('groups', 'seq'), parts along dimension 0, may hold values from -4 to 250
- atom_proj: bfloat16 [6, 4, 128, 128], replicated, may hold values from -0.5 to 0.5
- atom_up: bfloat16 [6, 2, 128, 256], replicated, may hold values from -0.5 to 0.5
- atom_down: bfloat16 [6, 256, 128], replicated, may hold values from -0.375 to 0.375
- atom_gains: float32 [6, 2, 128], replicated, may hold values from 0.5 to 1.5
- to_token: bfloat16 [128, 768], replicated, may hold values from -0.5 to 0.5
- token_proj: bfloat16 [4, 768, 768], replicated, may hold values from -0.21875 to 0.21875
- token_gain: float32 [768], replicated, may hold values from 0.5 to 2
- to_atom: bfloat16 [768, 128], replicated, may hold values from -0.21875 to 0.21875
Outputs:
- atoms_out: bfloat16 [2, 8192, 128], P('groups', 'seq'), parts along dimension 0
The draws below stay inside these ranges and needn't reach their ends.
There are 2 independent parts, one for each index of `groups`. The reference program is written for one: setup_inputs(seed, part) draws one part's arguments, and reference() takes and returns one part's arrays. A program takes and returns all parts, laid end to end along the dimension named above; an argument that names none is the same for every part. Nothing has to cross between parts.
Inputs may be any that keep to these rules, and one draw needn't show every extreme that they name: Token t lies in block d = t // 64; its atoms token_start[t] .. token_start[t] + token_len[t] - 1 lie within atoms (d - 1) * 512 .. (d + 2) * 512 - 1 and within the complex. Ranges of the tokens of one block are disjoint and rise with t; ranges of different blocks may share atoms; atoms may belong to no token. `token_len`: every block of 64 tokens has a token of exactly 12 atoms.
All inputs are finite; a program needn't handle non-finite values. No bound on the sum of `atom_mask` on one device may be relied on, other than what follows from the above.
Results may differ from the reference program's by a relative error of at most 0.024.
Values may be sent and summed in bfloat16 or wider, within the bound.
A program may use at most 128 MiB of HBM per device.

```python
import math
import jax
import jax.numpy as jnp
from jax import lax

S = 1
TOK_DEV = 64
MOSTLEN = 12
CA = 128
CT = 768
HT = 16
HA = 4
ATRANS = 256
WQ = 32
WK = 128
ENC_LAYERS = 3
DEC_LAYERS = 3
BLOCKS = 6
AT_DEV = 512
TOKENS = 1024
ATOMS = 8192


def token_ranges(key):
    blocks = TOKENS // TOK_DEV
    lengths = jax.random.randint(jax.random.fold_in(key, 11), (blocks, TOK_DEV), 1, MOSTLEN + 1)
    place = jax.random.randint(jax.random.fold_in(key, 13), (blocks, 1), 0, TOK_DEV)
    lengths = jnp.where(jnp.arange(TOK_DEV)[None, :] == place, MOSTLEN, lengths)
    shifts = jax.random.randint(jax.random.fold_in(key, 12), (blocks,), -(AT_DEV // 2), AT_DEV // 2)
    block_ids = jnp.arange(blocks)
    shifts = jnp.where(block_ids == 0, 0, shifts)
    shifts = jnp.where(block_ids == blocks - 1, -(AT_DEV // 2), shifts)
    inside = jnp.cumsum(lengths, axis=1) - lengths
    starts = block_ids[:, None] * AT_DEV + shifts[:, None] + inside
    return (starts.reshape(-1).astype(jnp.int32), lengths.reshape(-1).astype(jnp.int32))


def biased(key, head_count, row_count, col_count):
    keys_all = jax.random.split(key, 1)
    entries = jnp.clip(jax.random.normal(keys_all[0], (head_count, row_count, col_count), jnp.float32), -4.0, 4.0)
    return entries


def draw_token_start(key, part):
    return token_ranges(key)[0]


def draw_token_len(key, part):
    return token_ranges(key)[1]


def draw_atom_bias(key, part):
    return biased(jax.random.fold_in(key, 21), HA, ATOMS, WK).astype(jnp.float32)


def draw_pair_bias(key, part):
    return biased(jax.random.fold_in(key, 22), HT, TOKENS, TOKENS).astype(jnp.bfloat16)


def touch_ends(values, rng, low, largest):
    spot = [jax.random.randint(jax.random.fold_in(rng, axis), (), 0, length) for axis, length in enumerate(values.shape)]
    main_axis = values.shape.index(max(values.shape))
    beside = spot[:main_axis] + [(spot[main_axis] + 1) % values.shape[main_axis]] + spot[main_axis + 1:]
    return values.at[tuple(spot)].set(low).at[tuple(beside)].set(largest)


def levels(stream_key, dims, shards, least, largest):
    def one(position, parts):
        steps = jax.random.uniform(jax.random.fold_in(jax.random.fold_in(stream_key, 6), position), (parts,), jnp.float32, least / len(shards), largest / len(shards))
        return jnp.repeat(jnp.exp(steps), dims[position] // parts).reshape((-1,) + (1,) * (len(dims) - position - 1))

    loudness = one(*shards[0])
    for cut in shards[1:]:
        loudness = loudness * one(*cut)
    return loudness


def gaussian(stream_key, dims, width, limit, pieces=(), kind=jnp.bfloat16):
    array = width * jax.random.normal(stream_key, dims, jnp.float32)
    if pieces:
        array = array * levels(stream_key, dims, pieces, -0.22, 0.18)
    return jnp.clip(array, -limit, limit).astype(kind)


def setup_inputs(seed: int = 0, part: int = 0) -> dict:
    key_list = jax.random.split(jax.random.key(seed), 16)
    part_keys = jax.random.split(jax.random.fold_in(key_list[15], part), 16)
    atoms = gaussian(part_keys[0], (S, ATOMS, CA), 1.0, 6.0, ((1, 16),))
    s_cond = gaussian(part_keys[1], (TOKENS, CT), 1.0, 6.0, ((0, 16),))
    token_start = draw_token_start(jax.random.fold_in(jax.random.fold_in(key_list[15], part), 71), part)
    token_len = draw_token_len(jax.random.fold_in(jax.random.fold_in(key_list[15], part), 71), part)
    atom_mask = touch_ends((jax.random.randint(part_keys[4], (ATOMS,), 0, 8) < 7).astype(jnp.int32), jax.random.fold_in(part_keys[4], 1), 0, 1)
    atom_bias = draw_atom_bias(jax.random.fold_in(jax.random.fold_in(key_list[15], part), 71), part)
    pair_bias = draw_pair_bias(jax.random.fold_in(jax.random.fold_in(key_list[15], part), 71), part)
    atom_proj = gaussian(key_list[7], (BLOCKS, 4, CA, CA), CA ** -0.5, 0.5)
    atom_up = gaussian(key_list[8], (BLOCKS, 2, CA, ATRANS), CA ** -0.5, 0.5)
    atom_down = gaussian(key_list[9], (BLOCKS, ATRANS, CA), ATRANS ** -0.5, 0.375)
    atom_gains = jnp.clip(1.0 + 0.1 * jax.random.normal(key_list[10], (BLOCKS, 2, CA), jnp.float32), 0.5, 1.5)
    to_token = gaussian(key_list[11], (CA, CT), CA ** -0.5, 0.5)
    token_proj = gaussian(key_list[12], (4, CT, CT), CT ** -0.5, 0.21875)
    token_gain = jnp.clip(jnp.exp(jax.random.uniform(key_list[13], (CT,), jnp.float32, math.log(0.5), math.log(2.0))), 0.5, 2.0)
    to_atom = gaussian(key_list[14], (CT, CA), CT ** -0.5, 0.21875)
    return dict(atoms=atoms, s_cond=s_cond, token_start=token_start, token_len=token_len, atom_mask=atom_mask, atom_bias=atom_bias, pair_bias=pair_bias, atom_proj=atom_proj, atom_up=atom_up, atom_down=atom_down, atom_gains=atom_gains, to_token=to_token, token_proj=token_proj, token_gain=token_gain, to_atom=to_atom)


epsilon = 1e-05
masked = -1000000000.0

def layer_norm(values, gain_vec):
    average = lax.optimization_barrier(jnp.mean(values, axis=-1, keepdims=True))
    centred = values - average
    spread = lax.optimization_barrier(jnp.mean(centred * centred, axis=-1, keepdims=True))
    return centred * lax.rsqrt(spread + epsilon) * gain_vec

def atom_block(stream, key_mask, bias_rows, proj_set, up_pair, down_proj, gain_pair):
    samples, atoms_all, channels = stream.shape
    rim = (WK - WQ) // 2
    head_size = channels // HA
    windows = atoms_all // WQ
    normed = layer_norm(stream, gain_pair[0]).astype(jnp.bfloat16)
    queries = jnp.dot(normed, proj_set[0], preferred_element_type=jnp.float32).astype(jnp.bfloat16)
    key_rows = jnp.dot(normed, proj_set[1], preferred_element_type=jnp.float32).astype(jnp.bfloat16)
    value_rows = jnp.dot(normed, proj_set[2], preferred_element_type=jnp.float32).astype(jnp.bfloat16)
    padded_keys = jnp.pad(key_rows, ((0, 0), (rim, rim), (0, 0)))
    padded_values = jnp.pad(value_rows, ((0, 0), (rim, rim), (0, 0)))
    key_index = (jnp.arange(windows, dtype=jnp.int32) * WQ)[:, None] + jnp.arange(WK, dtype=jnp.int32)[None, :]
    window_mask = jnp.pad(key_mask, (rim, rim))[key_index]
    query_win = queries.reshape(samples, windows, WQ, HA, head_size).astype(jnp.float32)
    keys_win = padded_keys[:, key_index].reshape(samples, windows, WK, HA, head_size).astype(jnp.float32)
    values_win = padded_values[:, key_index].reshape(samples, windows, WK, HA, head_size).astype(jnp.float32)
    scores = jnp.einsum('snqhd,snkhd->snhqk', query_win, keys_win)
    bias_terms = bias_rows.reshape(HA, windows, WQ, WK).transpose(1, 0, 2, 3)[None]
    logits = scores * head_size ** (-0.5) + bias_terms + jnp.where(window_mask == 1, 0.0, masked)[None, :, None, None, :]
    weights = jax.nn.softmax(logits, axis=-1).astype(jnp.bfloat16)
    mixture = jnp.einsum('snhqk,snkhd->snqhd', weights.astype(jnp.float32), values_win)
    mixture = mixture.astype(jnp.bfloat16).reshape(samples, atoms_all, channels)
    stream = stream + jnp.dot(mixture, proj_set[3], preferred_element_type=jnp.float32)
    second = layer_norm(stream, gain_pair[1]).astype(jnp.bfloat16)
    gated = jax.nn.silu(jnp.dot(second, up_pair[0], preferred_element_type=jnp.float32))
    hidden = (gated * jnp.dot(second, up_pair[1], preferred_element_type=jnp.float32)).astype(jnp.bfloat16)
    return stream + jnp.dot(hidden, down_proj, preferred_element_type=jnp.float32)

def block_members(block_id, token_start, token_len):
    window = 3 * AT_DEV
    first_atom = jnp.clip((block_id - 1) * AT_DEV, 0, ATOMS - window).astype(jnp.int32)
    starts = lax.dynamic_slice_in_dim(token_start, (block_id * TOK_DEV).astype(jnp.int32), TOK_DEV)
    lengths = lax.dynamic_slice_in_dim(token_len, (block_id * TOK_DEV).astype(jnp.int32), TOK_DEV)
    positions = first_atom + jnp.arange(window, dtype=jnp.int32)
    member = (positions[None, :] >= starts[:, None]) & (positions[None, :] < (starts + lengths)[:, None])
    return (first_atom, member.astype(jnp.float32), lengths)

def reference(atoms, s_cond, token_start, token_len, atom_mask, atom_bias, pair_bias, atom_proj, atom_up, atom_down, atom_gains, to_token, token_proj, token_gain, to_atom):
    stream = atoms.astype(jnp.float32)
    for block_id in range(ENC_LAYERS):
        stream = atom_block(stream, atom_mask, atom_bias, atom_proj[block_id], atom_up[block_id], atom_down[block_id], atom_gains[block_id])
    encoded = stream.astype(jnp.bfloat16)
    window = 3 * AT_DEV
    block_count = TOKENS // TOK_DEV

    def pool_block(block_id):
        block_id = block_id.astype(jnp.int32)
        first_atom, member, lengths = block_members(block_id, token_start, token_len)
        part_atoms = lax.dynamic_slice_in_dim(encoded, first_atom, window, 1)
        projected = jax.nn.relu(jnp.dot(part_atoms, to_token, preferred_element_type=jnp.float32)).astype(jnp.bfloat16)
        totals = jnp.einsum('ta,sac->stc', member, projected.astype(jnp.float32))
        return totals / lengths[None, :, None].astype(jnp.float32)
    pooled = lax.map(pool_block, jnp.arange(block_count, dtype=jnp.int32))
    features = pooled.transpose(1, 0, 2, 3).reshape(S, TOKENS, CT) + s_cond.astype(jnp.float32)[None]
    normed = layer_norm(features, token_gain).astype(jnp.bfloat16)
    queries = jnp.dot(normed, token_proj[0], preferred_element_type=jnp.float32).astype(jnp.bfloat16)
    key_rows = jnp.dot(normed, token_proj[1], preferred_element_type=jnp.float32).astype(jnp.bfloat16)
    value_rows = jnp.dot(normed, token_proj[2], preferred_element_type=jnp.float32).astype(jnp.bfloat16)
    head_size = CT // HT

    def attend(sample_rows):
        query_one, key_one, value_one = sample_rows
        query_h = query_one.reshape(TOKENS, HT, head_size).astype(jnp.float32).transpose(1, 0, 2)
        key_h = key_one.reshape(TOKENS, HT, head_size).astype(jnp.float32).transpose(1, 0, 2)
        value_h = value_one.reshape(TOKENS, HT, head_size).astype(jnp.float32).transpose(1, 0, 2)

        def one_head(head_rows):
            query_x, key_x, value_x, bias_x = head_rows
            scores = jnp.dot(query_x, key_x.T)
            logits = scores * head_size ** (-0.5) + bias_x.astype(jnp.float32)
            weights = jax.nn.softmax(logits, axis=-1).astype(jnp.bfloat16)
            return jnp.dot(weights.astype(jnp.float32), value_x)
        mixture = lax.map(one_head, (query_h, key_h, value_h, pair_bias))
        return mixture.transpose(1, 0, 2).astype(jnp.bfloat16).reshape(TOKENS, CT)
    token_mix = lax.map(attend, (queries, key_rows, value_rows))
    updated = features + jnp.dot(token_mix, token_proj[3], preferred_element_type=jnp.float32)
    atom_rows = jnp.dot(updated.astype(jnp.bfloat16), to_atom, preferred_element_type=jnp.float32).astype(jnp.bfloat16)

    def spread_block(block_id, running):
        block_id = jnp.asarray(block_id).astype(jnp.int32)
        first_atom, member, lengths = block_members(block_id, token_start, token_len)
        rows_block = lax.dynamic_slice_in_dim(atom_rows, (block_id * TOK_DEV).astype(jnp.int32), TOK_DEV, 1)
        contrib = jnp.einsum('ta,stc->sac', member, rows_block.astype(jnp.float32))
        current = lax.dynamic_slice_in_dim(running, first_atom, window, 1)
        return lax.dynamic_update_slice_in_dim(running, current + contrib, first_atom, 1)
    returned = lax.fori_loop(0, block_count, spread_block, jnp.zeros((S, ATOMS, CA), jnp.float32))
    stream = stream + returned
    for block_id in range(ENC_LAYERS, ENC_LAYERS + DEC_LAYERS):
        stream = atom_block(stream, atom_mask, atom_bias, atom_proj[block_id], atom_up[block_id], atom_down[block_id], atom_gains[block_id])
    return stream.astype(jnp.bfloat16)
```

```python
import functools

import jax
import jax.numpy as jnp
from jax import lax
from jax.experimental import pallas as pl
from jax.experimental.pallas import tpu as pltpu
from jax.sharding import PartitionSpec as P

HT = 16
HA = 4
WQ = 32
WK = 128
HALF = 3
RIM = (WK - WQ) // 2
LANES = 128
SPARE = (4, 2, 0)
EDGE = SPARE[0] * WQ
PAD = EDGE + RIM
KEPT = (SPARE[1] * WQ + RIM, RIM, 0)

epsilon = 1e-05
masked = -1000000000.0
LOG2E = 1.4426950408889634
MESH = pl.DeviceIdType.MESH
F32 = jnp.float32
BF16 = jnp.bfloat16

MASK, RANGE, ATOMS, BIAS, ENC, ROWS = 0, 1, 2, 3, 4, 6
ENC_PARTS = 2


def layer_norm(values, gain_vec):
    average = jnp.mean(values, axis=-1, keepdims=True)
    centred = values - average
    spread = jnp.mean(centred * centred, axis=-1, keepdims=True)
    return centred * lax.rsqrt(spread + epsilon) * gain_vec


def mm(left, right):
    return jnp.dot(left, right, preferred_element_type=F32)


def mm_nt(left, right):
    return lax.dot_general(left, right, (((1,), (1,)), ((), ())), preferred_element_type=F32)


def head_mask(rows, row_size, cols, col_size):
    row_head = lax.broadcasted_iota(jnp.int32, (rows, cols), 0) // row_size
    col_head = lax.broadcasted_iota(jnp.int32, (rows, cols), 1) // col_size
    return row_head == col_head


def pieces(low, high, most):
    units = (high - low) // 16
    number = pl.cdiv(high - low, most)
    marks = [low + 16 * (units * i // number) for i in range(number)] + [high]
    return list(zip(marks[:-1], marks[1:]))


def kernel(
    count,
    atoms_hbm,
    s_cond_hbm,
    start_ref,
    length_ref,
    mask_ref,
    bias_hbm,
    pair_hbm,
    proj_hbm,
    up_hbm,
    down_hbm,
    gains_ref,
    to_token_hbm,
    token_proj_hbm,
    token_gain_ref,
    to_atom_hbm,
    out_hbm,
    atx_ref,
    x_ref,
    kv_ref,
    q_ref,
    mix_ref,
    bias_ref,
    pair_ref,
    qkv_w,
    o_w,
    up_ref,
    down_ref,
    to_token_ref,
    to_atom_ref,
    s_cond_ref,
    tp_ref,
    mex_ref,
    wt_ref,
    lg_ref,
    rngx_ref,
    encx_ref,
    rowsx_ref,
    uall_ref,
    feat_ref,
    qk_ref,
    acc_ref,
    max_ref,
    out_ref,
    load_sem,
    out_sem,
    side_send,
    side_recv,
    far_send,
    far_recv,
    z_send,
    y_send,
    c_send,
    u_recv,
):
    me = lax.axis_index("seq")
    core = lax.rem(me, 2)
    row_y = lax.rem(me // 2, 2)
    row_z = me // 4
    depth = count // 4
    atoms_dev = atoms_hbm.shape[1]
    channels = atoms_hbm.shape[2]
    tokens_dev, width = s_cond_ref.shape
    windows = atoms_dev // WQ
    head_size = channels // HA
    token_head = width // HT
    core_peer = me + 1 - 2 * core
    y_peer = me + 2 - 4 * row_y
    own = slice(PAD, PAD + atoms_dev)
    bias_rows = EDGE - WQ + RIM % WQ

    def there(offset):
        return me + offset >= 0 if offset < 0 else me + offset < count

    barrier = pltpu.get_barrier_semaphore()

    def greet(target):
        pl.semaphore_signal(barrier, inc=1, device_id={"seq": target}, device_id_type=MESH)

    for offset in (-1, 1, -2, 2):
        pl.when(there(offset))(lambda: greet(me + offset))
    for z in range(depth):
        pl.when(row_z != z)(lambda: greet(me + 4 * (z - row_z)))

    def load(index, source, target):
        copy = pltpu.make_async_copy(source, target, load_sem.at[index])
        copy.start()
        return copy

    atoms_load = load(0, atoms_hbm.at[0], atx_ref.at[pl.ds(PAD, atoms_dev)])
    qkv_loads = [
        load(1 + k, proj_hbm.at[:, k], qkv_w.at[:, :, pl.ds(k * channels, channels)]) for k in range(3)
    ]
    bias_load = load(4, bias_hbm, bias_ref.at[:, pl.ds(EDGE, atoms_dev)])
    o_load = load(5, proj_hbm.at[:, 3], o_w)
    up_load = load(6, up_hbm, up_ref)
    down_load = load(7, down_hbm, down_ref)
    pool_loads = [load(8, to_token_hbm, to_token_ref), load(9, s_cond_hbm, s_cond_ref)]
    tp_load = load(10, token_proj_hbm, tp_ref)
    pair_load = load(11, pair_hbm, pair_ref)
    to_atom_load = load(12, to_atom_hbm, to_atom_ref)

    mex_ref[1] = mask_ref[...].reshape(mex_ref.shape[1:])
    starts = start_ref[...].reshape(1, tokens_dev)
    rngx_ref[2, 0:1, 0:tokens_dev] = starts
    rngx_ref[2, 1:2, 0:tokens_dev] = starts + length_ref[...].reshape(1, tokens_dev)

    def zero(ref, slot):
        ref[slot] = jnp.zeros(ref.shape[1:], ref.dtype)

    def clear_near(side):
        for ref in (mex_ref, encx_ref):
            zero(ref, 2 * side)
        for ref in (rngx_ref, rowsx_ref):
            zero(ref, 1 + 2 * side)
        rows = slice(0, PAD) if side == 0 else slice(PAD + atoms_dev, 2 * PAD + atoms_dev)
        atx_ref[rows] = jnp.zeros((PAD, channels), BF16)
        rows = slice(0, EDGE) if side == 0 else slice(EDGE + atoms_dev, 2 * EDGE + atoms_dev)
        bias_ref[:, rows] = jnp.zeros((HA, EDGE, WK), F32)

    def clear_far(side):
        for ref in (rngx_ref, rowsx_ref):
            zero(ref, 4 * side)

    for side in range(2):
        sign = 2 * side - 1
        pl.when(jnp.logical_not(there(sign)))(lambda: clear_near(side))
        pl.when(jnp.logical_not(there(2 * sign)))(lambda: clear_far(side))
    bias_ref[:, 0 : EDGE - bias_rows] = jnp.zeros((HA, EDGE - bias_rows, WK), F32)
    bias_ref[:, EDGE + atoms_dev + bias_rows :] = jnp.zeros((HA, EDGE - bias_rows, WK), F32)

    class Sides:
        def __init__(self, reach, send, recv, to_left, to_right):
            self.reach = reach
            self.copies = [
                pltpu.make_async_remote_copy(
                    source, target, send(i), recv(i), device_id={"seq": me + sign * reach}, device_id_type=MESH
                )
                for i, (sign, (source, target)) in enumerate(zip((-1, 1), (to_left, to_right)))
            ]

        def start(self):
            pl.when(there(-self.reach))(lambda: self.copies[0].start())
            pl.when(there(self.reach))(lambda: self.copies[1].start())

        def receive(self):
            pl.when(there(self.reach))(lambda: self.copies[0].wait_recv())
            pl.when(there(-self.reach))(lambda: self.copies[1].wait_recv())

        def sent(self):
            pl.when(there(-self.reach))(lambda: self.copies[0].wait_send())
            pl.when(there(self.reach))(lambda: self.copies[1].wait_send())

    def near(kind, to_left, to_right):
        return Sides(1, lambda i: side_send.at[kind, i], lambda i: side_recv.at[kind, i], to_left, to_right)

    def far(kind, to_left, to_right):
        return Sides(2, lambda i: far_send.at[kind, i], lambda i: far_recv.at[kind, i], to_left, to_right)

    mask_sides = near(MASK, (mex_ref.at[1], mex_ref.at[2]), (mex_ref.at[1], mex_ref.at[0]))
    range_sides = near(RANGE, (rngx_ref.at[2], rngx_ref.at[3]), (rngx_ref.at[2], rngx_ref.at[1]))
    range_far = far(0, (rngx_ref.at[2], rngx_ref.at[4]), (rngx_ref.at[2], rngx_ref.at[0]))
    row_sides = near(ROWS, (rowsx_ref.at[2], rowsx_ref.at[3]), (rowsx_ref.at[2], rowsx_ref.at[1]))
    row_far = far(1, (rowsx_ref.at[2], rowsx_ref.at[4]), (rowsx_ref.at[2], rowsx_ref.at[0]))
    atom_sides = near(
        ATOMS,
        (atoms_hbm.at[0, pl.ds(0, PAD)], atx_ref.at[pl.ds(PAD + atoms_dev, PAD)]),
        (atoms_hbm.at[0, pl.ds(atoms_dev - PAD, PAD)], atx_ref.at[pl.ds(0, PAD)]),
    )
    bias_sides = near(
        BIAS,
        (bias_hbm.at[:, pl.ds(0, bias_rows)], bias_ref.at[:, pl.ds(EDGE + atoms_dev, bias_rows)]),
        (
            bias_hbm.at[:, pl.ds(atoms_dev - bias_rows, bias_rows)],
            bias_ref.at[:, pl.ds(EDGE - bias_rows, bias_rows)],
        ),
    )
    enc_size = atoms_dev // ENC_PARTS

    def enc_part(part):
        rows = pl.ds(part * enc_size, enc_size)
        return near(
            ENC + part,
            (encx_ref.at[1, rows], encx_ref.at[2, rows]),
            (encx_ref.at[1, rows], encx_ref.at[0, rows]),
        )

    enc_sides = [enc_part(part) for part in range(ENC_PARTS)]

    mask_lines = atoms_dev // LANES

    def mask_row(index):
        return mex_ref[index // mask_lines, index % mask_lines : index % mask_lines + 1, :]

    def window_mask(window):
        first = atoms_dev + window * WQ - RIM
        row, offset = first // LANES, first % LANES
        line = mask_row(row)
        if offset:
            line = jnp.concatenate([line[:, offset:], mask_row(row + 1)[:, :offset]], axis=1)
        return jnp.where(line == 1, 0.0, masked).astype(F32)

    atom_heads = head_mask(HA * WQ, WQ, channels, head_size)


    both_heads = jnp.concatenate([atom_heads] * 2, axis=1)

    def score(layer, window, fresh):
        first = PAD + window * WQ
        query = q_ref[first : first + WQ, :]
        tall = jnp.where(atom_heads, jnp.concatenate([query] * HA, axis=0), jnp.zeros((), BF16))
        keys = kv_ref[0, first - RIM : first - RIM + WK, :]
        rows = slice(EDGE + window * WQ, EDGE + window * WQ + WQ)
        bias = bias_ref[:, rows, :]
        if fresh:
            bias = (bias + window_mask(window)) * LOG2E
            bias_ref[:, rows, :] = bias
        return mm_nt(tall, keys) + bias.reshape(HA * WQ, WK)

    def soft(logits):
        return jnp.exp2(logits - jnp.max(logits, axis=-1, keepdims=True)).astype(BF16)

    def mix(window, weights):
        first = PAD + window * WQ
        values = jnp.concatenate(
            [kv_ref[1, first - RIM : first - RIM + WK, :], jnp.ones((WK, channels), BF16)], axis=1
        )
        both = jnp.where(both_heads, mm(weights, values), 0.0)
        joined = both[0:WQ]
        for head in range(1, HA):
            joined = joined + both[head * WQ : (head + 1) * WQ]
        mix_ref[first : first + WQ, :] = (joined[:, :channels] / joined[:, channels:]).astype(BF16)

    def attend_all(layer, which, fresh=False):
        for window in which:
            wt_ref[window + SPARE[0]] = soft(score(layer, window, fresh))
        for window in which:
            mix(window, wt_ref[window + SPARE[0]])

    def project(layer, low, high):
        gain = gains_ref[layer]
        for a, b in pieces(low, high, 128):
            normed = layer_norm(x_ref[a:b], gain[0:1]).astype(BF16)
            three = mm(normed, qkv_w[layer])
            q_ref[a:b] = (three[:, :channels] * (LOG2E * head_size ** (-0.5))).astype(BF16)
            for kind in range(2):
                kv_ref[kind, a:b] = three[:, (kind + 1) * channels : (kind + 2) * channels].astype(BF16)

    def transition(layer, a, b):
        gain = gains_ref[layer]
        stream = x_ref[a:b] + mm(mix_ref[a:b], o_w[layer])
        second = layer_norm(stream, gain[1:2]).astype(BF16)
        gate = 0.5 * mm(second, up_ref[layer, 0])
        gated = gate + gate * jnp.tanh(gate)
        hidden = (gated * mm(second, up_ref[layer, 1])).astype(BF16)
        return stream + mm(hidden, down_ref[layer])

    def advance(layer, low, high):
        for a, b in pieces(low, high, 1024):
            x_ref[a:b] = transition(layer, a, b)

    def outside():
        def left():
            x_ref[0:PAD] = jnp.zeros((PAD, channels), F32)

        def right():
            x_ref[PAD + atoms_dev :] = jnp.zeros((PAD, channels), F32)

        pl.when(jnp.logical_not(there(-1)))(left)
        pl.when(jnp.logical_not(there(1)))(right)

    def whole(layer, step):
        spare, kept = SPARE[step], KEPT[step]
        project(layer, PAD - spare * WQ - RIM, PAD + atoms_dev + spare * WQ + RIM)
        attend_all(layer, range(-spare, windows + spare))
        advance(layer, PAD - kept, PAD + atoms_dev + kept)
        outside()

    def last(layer, parts, finish):
        project(layer, PAD - RIM, PAD + atoms_dev + RIM)
        size = atoms_dev // parts
        for part in range(parts):
            attend_all(layer, range(part * size // WQ, (part + 1) * size // WQ))
            finish(part, part * size, size, transition(layer, PAD + part * size, PAD + (part + 1) * size))

    atoms_load.wait()
    for copy in qkv_loads:
        copy.wait()
    x_ref[own] = atx_ref[own].astype(F32)
    project(0, PAD, PAD + atoms_dev)

    peers = (depth - 1) + sum(jnp.where(there(offset), 1, 0) for offset in (-1, 1, -2, 2))
    pl.semaphore_wait(barrier, peers)
    for sides in (mask_sides, atom_sides, bias_sides, range_sides, range_far):
        sides.start()
    bias_load.wait()
    inner = range(RIM // WQ + 1, windows - RIM // WQ - 1)
    attend_all(0, inner, fresh=True)
    mask_sides.receive()
    atom_sides.receive()
    for a in (0, PAD + atoms_dev):
        x_ref[a : a + PAD] = atx_ref[a : a + PAD].astype(F32)
        project(0, a, a + PAD)
    attend_all(0, [w for w in range(windows) if w not in inner], fresh=True)
    o_load.wait()
    up_load.wait()
    down_load.wait()
    advance(0, PAD, PAD + atoms_dev)
    bias_sides.receive()
    attend_all(0, [w for w in range(-SPARE[0], windows + SPARE[0]) if w < 0 or w >= windows], fresh=True)
    advance(0, PAD - KEPT[0], PAD)
    advance(0, PAD + atoms_dev, PAD + atoms_dev + KEPT[0])
    outside()
    whole(1, 1)

    def encoded(part, first, size, rows):
        x_ref[PAD + first : PAD + first + size] = rows
        encx_ref[1, first : first + size] = rows.astype(BF16)
        enc_sides[part].start()

    last(2, ENC_PARTS, encoded)

    range_sides.receive()
    range_far.receive()
    for copy in pool_loads:
        copy.wait()
    eye = head_mask(tokens_dev, 1, tokens_dev, 1)

    def column(line):
        return jnp.sum(jnp.where(eye, line.astype(F32), 0.0), axis=1, keepdims=True)

    start_col = column(rngx_ref[2, 0:1, 0:tokens_dev])
    end_col = column(rngx_ref[2, 1:2, 0:tokens_dev])

    def pooled(block):
        projected = jnp.maximum(mm(encx_ref[block], to_token_ref[...]), 0.0).astype(BF16)
        place = (me + block - 1) * atoms_dev + lax.broadcasted_iota(
            jnp.int32, (tokens_dev, atoms_dev), 1
        )
        place = place.astype(F32)
        member = jnp.where((place >= start_col) & (place < end_col), 1.0, 0.0).astype(BF16)
        return mm(member, projected)

    totals = pooled(1)
    for sides in enc_sides:
        sides.receive()
    totals = totals + pooled(0) + pooled(2)
    features = totals / (end_col - start_col) + s_cond_ref[...].astype(F32)
    feat_ref[...] = features
    uall_ref[me] = layer_norm(features, token_gain_ref[...].reshape(1, width)).astype(BF16)

    def at(z, y, c):
        return (z * 2 + y) * 2 + c

    def u_copy(index, target, send):
        return pltpu.make_async_remote_copy(
            uall_ref.at[index],
            uall_ref.at[index],
            send,
            u_recv.at[index],
            device_id={"seq": target},
            device_id_type=MESH,
        )

    def u_arrived(index):
        u_copy(index, core_peer, c_send.at[0, 0]).wait_recv()

    def z_copy(z):
        return u_copy(me, at(z, row_y, core), z_send.at[z])

    def y_copy(z):
        return u_copy(at(z, row_y, core), y_peer, y_send.at[z])

    def c_copy(z, kind):
        return u_copy(at(z, (row_y + kind) % 2, core), core_peer, c_send.at[kind, z])

    shorter = jnp.minimum(row_z, depth - 1 - row_z)
    upward = jnp.where(depth - 1 - row_z > row_z, 1, -1)

    def order(step):
        turn = jnp.where(step % 2 == 1, (step + 1) // 2, -(step // 2))
        return row_z + jnp.where(step <= 2 * shorter, turn, upward * (step - shorter))

    y_copy(row_z).start()
    for step in range(1, depth):
        z_copy(order(step)).start()
    c_copy(row_z, 0).start()

    def relay(z):
        u_arrived(at(z, row_y, core))
        y_copy(z).start()
        c_copy(z, 0).start()

    tp_load.wait()
    half = HT // 2
    half_width = width // 2
    token_heads = head_mask(half * tokens_dev, tokens_dev, half_width, token_head)
    for part in range(2):
        cols = slice(part * half_width, (part + 1) * half_width)
        query = mm(uall_ref[me], tp_ref[0, :, cols]).astype(BF16)
        apart = jnp.where(
            token_heads, jnp.concatenate([query] * half, axis=0), jnp.zeros((), BF16)
        )
        qk_ref[part] = (mm_nt(apart, tp_ref[1, :, cols]) * token_head ** (-0.5)).astype(BF16)
    max_ref[...] = jnp.full_like(max_ref, -1e30)
    acc_ref[...] = jnp.zeros_like(acc_ref)
    pair_load.wait()
    span = 4 * tokens_dev

    def token_block(z):
        rows = uall_ref[pl.ds(4 * z, 4)].reshape(span, width)
        first = pl.multiple_of(z * span, span)
        for part in range(2):
            cols = slice(part * half_width, (part + 1) * half_width)
            values = mm(rows, tp_ref[2, :, cols]).astype(BF16)
            values = jnp.concatenate([values, jnp.ones((span, LANES), BF16)], axis=1)
            bias = pair_ref[part * half : (part + 1) * half, :, pl.ds(first, span)]
            bias = bias.reshape(half * tokens_dev, span).astype(F32)
            logits = mm_nt(qk_ref[part], rows) + bias
            before = max_ref[part][:, 0:1]
            now = jnp.maximum(before, jnp.max(logits, axis=-1, keepdims=True))
            weights = jnp.exp(logits - now)
            shrink = jnp.exp(before - now)
            acc_ref[part] = acc_ref[part] * shrink + mm(weights.astype(BF16), values)
            max_ref[part] = jnp.broadcast_to(now, max_ref.shape[1:])

    if depth > 1:
        relay(order(1))

    def token_step(step, carry):
        z = order(step)

        def ahead():
            relay(order(step + 2))

        pl.when(step + 2 < depth)(ahead)
        u_arrived(at(z, 1 - row_y, core))
        c_copy(z, 1).start()
        u_arrived(at(z, row_y, 1 - core))
        u_arrived(at(z, 1 - row_y, 1 - core))
        token_block(z)
        return carry

    lax.fori_loop(0, depth, token_step, 0)

    parts = []
    for part in range(2):
        mixed = acc_ref[part, :, 0:half_width] * (1.0 / acc_ref[part, :, half_width : half_width + 1])
        mixed = jnp.where(token_heads, mixed, 0.0)
        joined = mixed[0:tokens_dev]
        for head in range(1, half):
            joined = joined + mixed[head * tokens_dev : (head + 1) * tokens_dev]
        parts.append(joined.astype(BF16))
    token_mix = jnp.concatenate(parts, axis=1)
    updated = feat_ref[...] + mm(token_mix, tp_ref[3])
    to_atom_load.wait()
    rowsx_ref[2] = mm(updated.astype(BF16), to_atom_ref[...]).astype(BF16)
    row_sides.start()
    row_far.start()

    areas = ((0, PAD, 0), (PAD, PAD + atoms_dev, 1), (PAD + atoms_dev, 2 * PAD + atoms_dev, 2))

    def members(low, high, slot):
        shape = (high - low, 3 * tokens_dev)
        place = me * atoms_dev + low - PAD + lax.broadcasted_iota(jnp.int32, shape, 0)
        place = place.astype(F32)
        first, end = (
            jnp.concatenate([rngx_ref[slot + i, k : k + 1, 0:tokens_dev] for i in range(3)], axis=1).astype(F32)
            for k in range(2)
        )
        return jnp.where((place >= first) & (place < end), 1.0, 0.0).astype(BF16)

    x_ref[0:PAD] = encx_ref[0, atoms_dev - PAD : atoms_dev].astype(F32)
    x_ref[PAD + atoms_dev :] = encx_ref[2, 0:PAD].astype(F32)
    belongs = [members(*area) for area in areas]
    row_sides.receive()
    row_far.receive()
    for belong, (low, high, slot) in zip(belongs, areas):
        tall_rows = rowsx_ref[slot : slot + 3].reshape(3 * tokens_dev, channels)
        x_ref[low:high] = x_ref[low:high] + mm(belong, tall_rows)

    whole(HALF, 0)
    whole(HALF + 1, 1)

    out_parts = 2
    out_size = atoms_dev // out_parts

    def out_copy(part):
        rows = pl.ds(part * out_size, out_size)
        return pltpu.make_async_copy(out_ref.at[rows], out_hbm.at[0, rows], out_sem.at[part])

    def decoded(part, first, size, rows):
        out_ref[first : first + size] = rows.astype(BF16)
        out_copy(part).start()

    last(HALF + 2, out_parts, decoded)

    for sides in (mask_sides, range_sides, range_far, atom_sides, bias_sides, row_sides, row_far, *enc_sides):
        sides.sent()
    for step in range(depth):
        z = order(step)
        if step > 0:
            z_copy(z).wait_send()
        y_copy(z).wait_send()
        c_copy(z, 0).wait_send()
        c_copy(z, 1).wait_send()
    for part in range(out_parts):
        out_copy(part).wait()


def shards(
    count,
    atoms,
    s_cond,
    token_start,
    token_len,
    atom_mask,
    atom_bias,
    pair_bias,
    atom_proj,
    atom_up,
    atom_down,
    atom_gains,
    to_token,
    token_proj,
    token_gain,
    to_atom,
):
    atoms_dev, channels = atoms.shape[1:]
    tokens_dev, width = s_cond.shape
    layers = 2 * HALF
    vmem = pl.BlockSpec(memory_space=pltpu.VMEM)
    hbm = pl.BlockSpec(memory_space=pl.ANY)
    half = HT // 2
    depth = count // 4
    spread = atoms_dev + 2 * PAD
    return pl.pallas_call(
        functools.partial(kernel, count),
        out_shape=jax.ShapeDtypeStruct(atoms.shape, BF16),
        in_specs=[hbm, hbm, vmem, vmem, vmem] + [hbm] * 5 + [vmem, hbm, hbm, vmem, hbm],
        out_specs=hbm,
        scratch_shapes=[
            pltpu.VMEM((spread, channels), BF16),
            pltpu.VMEM((spread, channels), F32),
            pltpu.VMEM((2, spread, channels), BF16),
            pltpu.VMEM((spread, channels), BF16),
            pltpu.VMEM((spread, channels), BF16),
            pltpu.VMEM((HA, atoms_dev + 2 * EDGE, WK), F32),
            pltpu.VMEM(pair_bias.shape, BF16),
            pltpu.VMEM((layers, channels, 3 * channels), BF16),
            pltpu.VMEM((layers, channels, channels), BF16),
            pltpu.VMEM(atom_up.shape, BF16),
            pltpu.VMEM(atom_down.shape, BF16),
            pltpu.VMEM(to_token.shape, BF16),
            pltpu.VMEM(to_atom.shape, BF16),
            pltpu.VMEM(s_cond.shape, BF16),
            pltpu.VMEM(token_proj.shape, BF16),
            pltpu.VMEM((3, atoms_dev // LANES, LANES), jnp.int32),
            pltpu.VMEM((atoms_dev // WQ + 2 * SPARE[0], HA * WQ, WK), BF16),
            pltpu.VMEM((atoms_dev // WQ + 2 * SPARE[0], HA * WQ, WK), F32),
            pltpu.VMEM((5, 8, pl.cdiv(tokens_dev, LANES) * LANES), jnp.int32),
            pltpu.VMEM((3, atoms_dev, channels), BF16),
            pltpu.VMEM((5, tokens_dev, channels), BF16),
            pltpu.VMEM((count, tokens_dev, width), BF16),
            pltpu.VMEM((tokens_dev, width), F32),
            pltpu.VMEM((2, half * tokens_dev, width), BF16),
            pltpu.VMEM((2, half * tokens_dev, width // 2 + LANES), F32),
            pltpu.VMEM((2, half * tokens_dev, LANES), F32),
            pltpu.VMEM((atoms_dev, channels), BF16),
            pltpu.SemaphoreType.DMA((13,)),
            pltpu.SemaphoreType.DMA((2,)),
            pltpu.SemaphoreType.DMA((7, 2)),
            pltpu.SemaphoreType.DMA((7, 2)),
            pltpu.SemaphoreType.DMA((2, 2)),
            pltpu.SemaphoreType.DMA((2, 2)),
            pltpu.SemaphoreType.DMA((depth,)),
            pltpu.SemaphoreType.DMA((depth,)),
            pltpu.SemaphoreType.DMA((2, depth)),
            pltpu.SemaphoreType.DMA((count,)),
        ],
        compiler_params=pltpu.CompilerParams(
            collective_id=0, has_side_effects=True, vmem_limit_bytes=60 * 1024 * 1024
        ),
    )(
        atoms,
        s_cond,
        token_start,
        token_len,
        atom_mask,
        atom_bias,
        pair_bias,
        atom_proj,
        atom_up,
        atom_down,
        atom_gains,
        to_token,
        token_proj,
        token_gain,
        to_atom,
    )


def solution(mesh):
    placed = (
        P("groups", "seq", None),
        P(("groups", "seq"), None),
        P(("groups", "seq")),
        P(("groups", "seq")),
        P(("groups", "seq")),
        P("groups", "seq", None),
        P("groups", "seq", None),
        P(),
        P(),
        P(),
        P(),
        P(),
        P(),
        P(),
        P(),
    )
    return jax.shard_map(
        functools.partial(shards, mesh.shape["seq"]),
        mesh=mesh,
        in_specs=placed,
        out_specs=P("groups", "seq", None),
        check_vma=False,
    )
```

```python
import functools

import jax
import jax.numpy as jnp
from jax import lax
from jax.experimental import pallas as pl
from jax.experimental.pallas import tpu as pltpu
from jax.sharding import PartitionSpec as P

HT = 16
HA = 4
WQ = 32
WK = 128
HALF = 3
RIM = (WK - WQ) // 2
LANES = 128
SPARE = (4, 2, 0)
EDGE = SPARE[0] * WQ
PAD = EDGE + RIM
KEPT = (SPARE[1] * WQ + RIM, RIM, 0)

epsilon = 1e-05
masked = -1000000000.0
LOG2E = 1.4426950408889634
MESH = pl.DeviceIdType.MESH
F32 = jnp.float32
BF16 = jnp.bfloat16

MASK, RANGE, ATOMS, BIAS, ENC, ROWS = 0, 1, 2, 3, 4, 6
ENC_PARTS = 2
REACH = (-1, 1, -2, 2)


def layer_norm(values, gain_vec):
    average = jnp.mean(values, axis=-1, keepdims=True)
    centred = values - average
    spread = jnp.mean(centred * centred, axis=-1, keepdims=True)
    return centred * lax.rsqrt(spread + epsilon) * gain_vec


def mm(left, right):
    return jnp.dot(left, right, preferred_element_type=F32)


def mm_nt(left, right):
    return lax.dot_general(left, right, (((1,), (1,)), ((), ())), preferred_element_type=F32)


def head_mask(rows, row_size, cols, col_size):
    row_head = lax.broadcasted_iota(jnp.int32, (rows, cols), 0) // row_size
    col_head = lax.broadcasted_iota(jnp.int32, (rows, cols), 1) // col_size
    return row_head == col_head


def pieces(low, high, most):
    units = (high - low) // 16
    number = pl.cdiv(high - low, most)
    marks = [low + 16 * (units * i // number) for i in range(number)] + [high]
    return list(zip(marks[:-1], marks[1:]))


def kernel(
    count,
    atoms_hbm,
    s_cond_hbm,
    start_ref,
    length_ref,
    mask_ref,
    bias_hbm,
    pair_hbm,
    proj_hbm,
    up_hbm,
    down_hbm,
    gains_ref,
    to_token_hbm,
    token_proj_hbm,
    token_gain_ref,
    to_atom_hbm,
    out_ref,
    atx_ref,
    x_ref,
    kv_ref,
    q_ref,
    mix_ref,
    bias_ref,
    shift_ref,
    beyond_ref,
    pair_ref,
    qkv_w,
    o_w,
    up_ref,
    down_ref,
    to_token_ref,
    to_atom_ref,
    s_cond_ref,
    tp_ref,
    mex_ref,
    wt_ref,
    rngx_ref,
    encx_ref,
    rowsx_ref,
    uall_ref,
    feat_ref,
    qk_ref,
    acc_ref,
    max_ref,
    load_sem,
    side_send,
    side_recv,
    far_send,
    far_recv,
    z_send,
    y_send,
    c_send,
    u_recv,
):
    me = lax.axis_index("seq")
    core = lax.rem(me, 2)
    row_y = lax.rem(me // 2, 2)
    row_z = me // 4
    depth = count // 4
    atoms_dev = atoms_hbm.shape[1]
    channels = atoms_hbm.shape[2]
    tokens_dev, width = s_cond_ref.shape
    windows = atoms_dev // WQ
    head_size = channels // HA
    token_head = width // HT
    core_peer = me + 1 - 2 * core
    y_peer = me + 2 - 4 * row_y
    own = slice(PAD, PAD + atoms_dev)
    bias_rows = EDGE - WQ + RIM % WQ

    def there(offset):
        return me + offset >= 0 if offset < 0 else me + offset < count

    barrier = pltpu.get_barrier_semaphore()

    def greet(target):
        pl.semaphore_signal(barrier, inc=1, device_id={"seq": target}, device_id_type=MESH)

    for offset in REACH:
        pl.when(there(offset))(lambda: greet(me + offset))
    for z in range(depth):
        pl.when(row_z != z)(lambda: greet(me + 4 * (z - row_z)))

    def load(index, source, target):
        copy = pltpu.make_async_copy(source, target, load_sem.at[index])
        copy.start()
        return copy

    atoms_load = load(0, atoms_hbm.at[0], atx_ref.at[pl.ds(PAD, atoms_dev)])
    qkv_loads = [
        load(1 + k, proj_hbm.at[:, k], qkv_w.at[:, :, pl.ds(k * channels, channels)]) for k in range(3)
    ]
    bias_load = load(4, bias_hbm, bias_ref.at[:, pl.ds(EDGE, atoms_dev)])
    o_load = load(5, proj_hbm.at[:, 3], o_w)
    up_load = load(6, up_hbm, up_ref)
    down_load = load(7, down_hbm, down_ref)
    pool_loads = [load(8, to_token_hbm, to_token_ref), load(9, s_cond_hbm, s_cond_ref)]
    tp_load = load(10, token_proj_hbm, tp_ref)
    pair_load = load(11, pair_hbm, pair_ref)
    to_atom_load = load(12, to_atom_hbm, to_atom_ref)

    mex_ref[1] = mask_ref[...].reshape(mex_ref.shape[1:])
    starts = start_ref[...].reshape(1, tokens_dev)
    rngx_ref[2, 0:1, 0:tokens_dev] = starts
    rngx_ref[2, 1:2, 0:tokens_dev] = starts + length_ref[...].reshape(1, tokens_dev)

    def zero(ref, slot):
        ref[slot] = jnp.zeros(ref.shape[1:], ref.dtype)

    def clear_near(side):
        for ref in (mex_ref, encx_ref):
            zero(ref, 2 * side)
        for ref in (rngx_ref, rowsx_ref):
            zero(ref, 1 + 2 * side)
        rows = slice(0, PAD) if side == 0 else slice(PAD + atoms_dev, 2 * PAD + atoms_dev)
        atx_ref[rows] = jnp.zeros((PAD, channels), BF16)
        zero(beyond_ref, side)

    def clear_far(side):
        for ref in (rngx_ref, rowsx_ref):
            zero(ref, 4 * side)

    for side in range(2):
        sign = 2 * side - 1
        pl.when(jnp.logical_not(there(sign)))(lambda: clear_near(side))
        pl.when(jnp.logical_not(there(2 * sign)))(lambda: clear_far(side))
    beyond_ref[0, :, 0 : EDGE - bias_rows] = jnp.zeros((HA, EDGE - bias_rows, WK), BF16)
    beyond_ref[1, :, bias_rows:] = jnp.zeros((HA, EDGE - bias_rows, WK), BF16)

    class Sides:
        def __init__(self, reach, send, recv, to_left, to_right):
            self.reach = reach
            self.copies = [
                pltpu.make_async_remote_copy(
                    source, target, send(i), recv(i), device_id={"seq": me + sign * reach}, device_id_type=MESH
                )
                for i, (sign, (source, target)) in enumerate(zip((-1, 1), (to_left, to_right)))
            ]

        def start(self):
            pl.when(there(-self.reach))(lambda: self.copies[0].start())
            pl.when(there(self.reach))(lambda: self.copies[1].start())

        def receive(self):
            pl.when(there(self.reach))(lambda: self.copies[0].wait_recv())
            pl.when(there(-self.reach))(lambda: self.copies[1].wait_recv())

        def sent(self):
            pl.when(there(-self.reach))(lambda: self.copies[0].wait_send())
            pl.when(there(self.reach))(lambda: self.copies[1].wait_send())

    def near(kind, to_left, to_right):
        return Sides(1, lambda i: side_send.at[kind, i], lambda i: side_recv.at[kind, i], to_left, to_right)

    def far(kind, to_left, to_right):
        return Sides(2, lambda i: far_send.at[kind, i], lambda i: far_recv.at[kind, i], to_left, to_right)

    mask_sides = near(MASK, (mex_ref.at[1], mex_ref.at[2]), (mex_ref.at[1], mex_ref.at[0]))
    range_sides = near(RANGE, (rngx_ref.at[2], rngx_ref.at[3]), (rngx_ref.at[2], rngx_ref.at[1]))
    range_far = far(0, (rngx_ref.at[2], rngx_ref.at[4]), (rngx_ref.at[2], rngx_ref.at[0]))
    row_sides = near(ROWS, (rowsx_ref.at[2], rowsx_ref.at[3]), (rowsx_ref.at[2], rowsx_ref.at[1]))
    row_far = far(1, (rowsx_ref.at[2], rowsx_ref.at[4]), (rowsx_ref.at[2], rowsx_ref.at[0]))
    atom_sides = near(
        ATOMS,
        (atoms_hbm.at[0, pl.ds(0, PAD)], atx_ref.at[pl.ds(PAD + atoms_dev, PAD)]),
        (atoms_hbm.at[0, pl.ds(atoms_dev - PAD, PAD)], atx_ref.at[pl.ds(0, PAD)]),
    )
    bias_sides = near(
        BIAS,
        (shift_ref.at[0], beyond_ref.at[1, :, pl.ds(0, bias_rows)]),
        (shift_ref.at[1], beyond_ref.at[0, :, pl.ds(EDGE - bias_rows, bias_rows)]),
    )
    enc_size = atoms_dev // ENC_PARTS

    def enc_part(part):
        rows = pl.ds(part * enc_size, enc_size)
        return near(
            ENC + part,
            (encx_ref.at[1, rows], encx_ref.at[2, rows]),
            (encx_ref.at[1, rows], encx_ref.at[0, rows]),
        )

    enc_sides = [enc_part(part) for part in range(ENC_PARTS)]

    mask_lines = atoms_dev // LANES

    def mask_row(index):
        return mex_ref[index // mask_lines, index % mask_lines : index % mask_lines + 1, :]

    def window_mask(window):
        first = atoms_dev + window * WQ - RIM
        row, offset = first // LANES, first % LANES
        line = mask_row(row)
        if offset:
            line = jnp.concatenate([line[:, offset:], mask_row(row + 1)[:, :offset]], axis=1)
        return jnp.where(line == 1, 0.0, masked).astype(F32)

    atom_heads = head_mask(HA * WQ, WQ, channels, head_size)


    both_heads = jnp.concatenate([atom_heads] * 2, axis=1)

    def score(layer, window, fresh):
        first = PAD + window * WQ
        query = q_ref[first : first + WQ, :]
        tall = jnp.where(atom_heads, jnp.concatenate([query] * HA, axis=0), jnp.zeros((), BF16))
        keys = kv_ref[0, first - RIM : first - RIM + WK, :]
        rows = slice(EDGE + window * WQ, EDGE + window * WQ + WQ)
        if fresh and not 0 <= window < windows:
            side, near_row = (0, EDGE + window * WQ) if window < 0 else (1, window * WQ - atoms_dev)
            bias = beyond_ref[side, :, near_row : near_row + WQ, :].astype(F32)
            bias = bias + window_mask(window) * LOG2E
            bias_ref[:, rows, :] = bias
        elif fresh:
            bias = (bias_ref[:, rows, :] + window_mask(window)) * LOG2E
            bias_ref[:, rows, :] = bias
        else:
            bias = bias_ref[:, rows, :]
        return mm_nt(tall, keys) + bias.reshape(HA * WQ, WK)

    def soft(logits):
        return jnp.exp2(logits - jnp.max(logits, axis=-1, keepdims=True)).astype(BF16)

    def mix(window, weights):
        first = PAD + window * WQ
        values = jnp.concatenate(
            [kv_ref[1, first - RIM : first - RIM + WK, :], jnp.ones((WK, channels), BF16)], axis=1
        )
        both = jnp.where(both_heads, mm(weights, values), 0.0)
        joined = both[0:WQ]
        for head in range(1, HA):
            joined = joined + both[head * WQ : (head + 1) * WQ]
        mix_ref[first : first + WQ, :] = (joined[:, :channels] / joined[:, channels:]).astype(BF16)

    def attend_all(layer, which, fresh=False):
        for window in which:
            wt_ref[window + SPARE[0]] = soft(score(layer, window, fresh))
        for window in which:
            mix(window, wt_ref[window + SPARE[0]])

    def rows_of(ref, ranges):
        parts = [ref[a:b] for a, b in ranges]
        return parts[0] if len(parts) == 1 else jnp.concatenate(parts, axis=0)

    def write_rows(ref, ranges, values):
        first = 0
        for a, b in ranges:
            ref[a:b] = values[first : first + b - a]
            first += b - a

    def project(layer, *ranges):
        gain = gains_ref[layer]
        for some in [ranges] if len(ranges) > 1 else [[piece] for piece in pieces(*ranges[0], 128)]:
            normed = layer_norm(rows_of(x_ref, some), gain[0:1]).astype(BF16)
            three = mm(normed, qkv_w[layer])
            write_rows(q_ref, some, (three[:, :channels] * (LOG2E * head_size ** (-0.5))).astype(BF16))
            for kind in range(2):
                write_rows(
                    kv_ref.at[kind], some, three[:, (kind + 1) * channels : (kind + 2) * channels].astype(BF16)
                )

    def transition(layer, *ranges):
        gain = gains_ref[layer]
        stream = rows_of(x_ref, ranges) + mm(rows_of(mix_ref, ranges), o_w[layer])
        second = layer_norm(stream, gain[1:2]).astype(BF16)
        gate = 0.5 * mm(second, up_ref[layer, 0])
        gated = gate + gate * jnp.tanh(gate)
        hidden = (gated * mm(second, up_ref[layer, 1])).astype(BF16)
        return stream + mm(hidden, down_ref[layer])

    def advance(layer, *ranges):
        write_rows(x_ref, ranges, transition(layer, *ranges))

    def outside():
        def left():
            x_ref[0:PAD] = jnp.zeros((PAD, channels), F32)

        def right():
            x_ref[PAD + atoms_dev :] = jnp.zeros((PAD, channels), F32)

        pl.when(jnp.logical_not(there(-1)))(left)
        pl.when(jnp.logical_not(there(1)))(right)

    def whole(layer, step):
        spare, kept = SPARE[step], KEPT[step]
        project(layer, (PAD - spare * WQ - RIM, PAD + atoms_dev + spare * WQ + RIM))
        attend_all(layer, range(-spare, windows + spare))
        advance(layer, (PAD - kept, PAD + atoms_dev + kept))
        outside()

    def last(layer, parts, finish):
        project(layer, (PAD - RIM, PAD + atoms_dev + RIM))
        size = atoms_dev // parts
        for part in range(parts):
            attend_all(layer, range(part * size // WQ, (part + 1) * size // WQ))
            finish(part, part * size, size, transition(layer, (PAD + part * size, PAD + (part + 1) * size)))

    atoms_load.wait()
    for copy in qkv_loads:
        copy.wait()
    x_ref[own] = atx_ref[own].astype(F32)
    project(0, (PAD, PAD + atoms_dev))

    bias_load.wait()
    for side, first in enumerate((EDGE, EDGE + atoms_dev - bias_rows)):
        rows = bias_ref[:, first : first + bias_rows, :]
        largest = jnp.max(rows, axis=-1, keepdims=True)
        shift_ref[side] = ((rows - largest) * LOG2E).astype(BF16)
    peers = (depth - 1) + sum(jnp.where(there(offset), 1, 0) for offset in REACH)
    pl.semaphore_wait(barrier, peers)
    for sides in (mask_sides, atom_sides, bias_sides, range_sides, range_far):
        sides.start()
    inner = range(RIM // WQ + 1, windows - RIM // WQ - 1)
    attend_all(0, inner, fresh=True)
    o_load.wait()
    up_load.wait()
    down_load.wait()
    begin, end = PAD + inner[0] * WQ, PAD + (inner[-1] + 1) * WQ
    advance(0, (begin, end))
    mask_sides.receive()
    atom_sides.receive()
    beside = ((0, PAD), (PAD + atoms_dev, 2 * PAD + atoms_dev))
    for a, b in beside:
        x_ref[a:b] = atx_ref[a:b].astype(F32)
    project(0, *beside)
    attend_all(0, [w for w in range(windows) if w not in inner], fresh=True)
    bias_sides.receive()
    attend_all(0, [w for w in range(-SPARE[0], windows + SPARE[0]) if w < 0 or w >= windows], fresh=True)
    advance(0, (PAD - KEPT[0], begin), (end, PAD + atoms_dev + KEPT[0]))
    outside()
    whole(1, 1)

    def encoded(part, first, size, rows):
        x_ref[PAD + first : PAD + first + size] = rows
        encx_ref[1, first : first + size] = rows.astype(BF16)
        enc_sides[part].start()

    last(2, ENC_PARTS, encoded)

    range_sides.receive()
    range_far.receive()
    for copy in pool_loads:
        copy.wait()
    eye = head_mask(tokens_dev, 1, tokens_dev, 1)

    def column(line):
        return jnp.sum(jnp.where(eye, line.astype(F32), 0.0), axis=1, keepdims=True)

    start_col = column(rngx_ref[2, 0:1, 0:tokens_dev])
    end_col = column(rngx_ref[2, 1:2, 0:tokens_dev])

    def pooled(block, low, size):
        projected = jnp.maximum(mm(encx_ref[block, low : low + size], to_token_ref[...]), 0.0).astype(BF16)
        place = (me + block - 1) * atoms_dev + low + lax.broadcasted_iota(
            jnp.int32, (tokens_dev, size), 1
        )
        place = place.astype(F32)
        member = jnp.where((place >= start_col) & (place < end_col), 1.0, 0.0).astype(BF16)
        return mm(member, projected)

    totals = pooled(1, 0, atoms_dev)
    for part in range(ENC_PARTS):
        enc_sides[part].receive()
        for block in (0, 2):
            totals = totals + pooled(block, part * enc_size, enc_size)
    features = totals / (end_col - start_col) + s_cond_ref[...].astype(F32)
    feat_ref[...] = features
    uall_ref[me] = layer_norm(features, token_gain_ref[...].reshape(1, width)).astype(BF16)

    def at(z, y, c):
        return (z * 2 + y) * 2 + c

    def u_copy(index, target, send):
        return pltpu.make_async_remote_copy(
            uall_ref.at[index],
            uall_ref.at[index],
            send,
            u_recv.at[index],
            device_id={"seq": target},
            device_id_type=MESH,
        )

    def u_arrived(index):
        u_copy(index, core_peer, c_send.at[0, 0]).wait_recv()

    def z_copy(z):
        return u_copy(me, at(z, row_y, core), z_send.at[z])

    def y_copy(z):
        return u_copy(at(z, row_y, core), y_peer, y_send.at[z])

    def c_copy(z, kind):
        return u_copy(at(z, (row_y + kind) % 2, core), core_peer, c_send.at[kind, z])

    shorter = jnp.minimum(row_z, depth - 1 - row_z)
    upward = jnp.where(depth - 1 - row_z > row_z, 1, -1)

    def order(step):
        turn = jnp.where(step % 2 == 1, (step + 1) // 2, -(step // 2))
        return row_z + jnp.where(step <= 2 * shorter, turn, upward * (step - shorter))

    def near_sends(step):
        z_copy(order(step)).start()

    at_end = shorter == 0
    inside = jnp.logical_not(at_end)
    y_copy(row_z).start()
    if depth > 1:
        near_sends(1)
    if depth > 2:
        pl.when(inside)(lambda: near_sends(2))
    c_copy(row_z, 0).start()

    def relay(z):
        u_arrived(at(z, row_y, core))
        y_copy(z).start()
        c_copy(z, 0).start()

    def across(z):
        u_arrived(at(z, 1 - row_y, core))
        c_copy(z, 1).start()

    tp_load.wait()
    half = HT // 2
    half_width = width // 2
    token_heads = head_mask(half * tokens_dev, tokens_dev, half_width, token_head)
    for part in range(2):
        cols = slice(part * half_width, (part + 1) * half_width)
        query = mm(uall_ref[me], tp_ref[0, :, cols]).astype(BF16)
        apart = jnp.where(
            token_heads, jnp.concatenate([query] * half, axis=0), jnp.zeros((), BF16)
        )
        folded = mm_nt(apart, tp_ref[1, :, cols]) * token_head ** (-0.5)
        qk_ref[part * half * tokens_dev : (part + 1) * half * tokens_dev] = folded.astype(BF16)
    max_ref[...] = jnp.full_like(max_ref, -1e30)
    acc_ref[...] = jnp.zeros_like(acc_ref)
    pair_load.wait()
    span = 4 * tokens_dev

    def token_block(places):
        rows = jnp.concatenate(
            [uall_ref[pl.ds(at(z, y, 0), 2)].reshape(2 * tokens_dev, width) for z, y in places], axis=0
        )
        bias = jnp.concatenate(
            [
                pair_ref[:, :, pl.ds(pl.multiple_of(at(z, y, 0) * tokens_dev, 2 * tokens_dev), 2 * tokens_dev)]
                for z, y in places
            ],
            axis=2,
        )
        bias = bias.reshape(HT * tokens_dev, span).astype(F32)
        logits = mm_nt(qk_ref[...], rows) + bias
        before = max_ref[...]
        now = jnp.maximum(before, jnp.max(logits, axis=-1, keepdims=True))
        max_ref[...] = now
        weights = jnp.exp(logits - jnp.concatenate([now] * (span // LANES), axis=1)).astype(BF16)
        shrink = jnp.exp(before - now)
        values = mm(rows, tp_ref[2]).astype(BF16)
        for part in range(2):
            cols = slice(part * half_width, (part + 1) * half_width)
            lines = slice(part * half * tokens_dev, (part + 1) * half * tokens_dev)
            mixed = mm(
                weights[lines], jnp.concatenate([values[:, cols], jnp.ones((span, LANES), BF16)], axis=1)
            )
            scale = jnp.concatenate([shrink[lines]] * (half_width // LANES + 1), axis=1)
            acc_ref[part] = acc_ref[part] * scale + mixed

    if depth > 1:
        z_copy(order(1)).wait_send()
    if depth > 2:
        pl.when(at_end)(lambda: near_sends(2))
    if depth > 3:
        pl.when(inside)(lambda: near_sends(3))
    across(order(0))
    if depth > 1:
        relay(order(1))

    def far_sends():
        z_copy(order(2)).wait_send()
        near_sends(3)

    if depth > 3:
        pl.when(at_end)(far_sends)
    for step in range(4, depth):
        near_sends(step)

    def other_core(step, kind):
        u_arrived(at(order(step), (row_y + kind) % 2, 1 - core))

    def token_pairs(step, kind):
        token_block([(order(step + i), (row_y + kind) % 2) for i in range(2)])

    def token_step(turn, carry):
        step = 2 * turn
        other_core(step, 0)
        other_core(step + 1, 0)
        token_pairs(step, 0)
        pl.when(step + 2 < depth)(lambda: relay(order(step + 2)))
        across(order(step + 1))
        pl.when(step + 3 < depth)(lambda: relay(order(step + 3)))
        other_core(step, 1)
        other_core(step + 1, 1)
        token_pairs(step, 1)
        pl.when(step + 2 < depth)(lambda: across(order(step + 2)))
        return carry

    lax.fori_loop(0, depth // 2, token_step, 0)

    parts = []
    for part in range(2):
        mixed = acc_ref[part, :, 0:half_width] * (1.0 / acc_ref[part, :, half_width : half_width + 1])
        mixed = jnp.where(token_heads, mixed, 0.0)
        joined = mixed[0:tokens_dev]
        for head in range(1, half):
            joined = joined + mixed[head * tokens_dev : (head + 1) * tokens_dev]
        parts.append(joined.astype(BF16))
    token_mix = jnp.concatenate(parts, axis=1)
    updated = feat_ref[...] + mm(token_mix, tp_ref[3])
    to_atom_load.wait()
    rowsx_ref[2] = mm(updated.astype(BF16), to_atom_ref[...]).astype(BF16)
    row_sides.start()
    row_far.start()

    areas = ((0, PAD, 0), (PAD, PAD + atoms_dev, 1), (PAD + atoms_dev, 2 * PAD + atoms_dev, 2))

    def members(low, high, slot):
        shape = (high - low, 3 * tokens_dev)
        place = me * atoms_dev + low - PAD + lax.broadcasted_iota(jnp.int32, shape, 0)
        place = place.astype(F32)
        first, end = (
            jnp.concatenate([rngx_ref[slot + i, k : k + 1, 0:tokens_dev] for i in range(3)], axis=1).astype(F32)
            for k in range(2)
        )
        return jnp.where((place >= first) & (place < end), 1.0, 0.0).astype(BF16)

    x_ref[0:PAD] = encx_ref[0, atoms_dev - PAD : atoms_dev].astype(F32)
    x_ref[PAD + atoms_dev :] = encx_ref[2, 0:PAD].astype(F32)
    belongs = [members(*area) for area in areas]
    row_sides.receive()
    row_far.receive()
    for belong, (low, high, slot) in zip(belongs, areas):
        tall_rows = rowsx_ref[slot : slot + 3].reshape(3 * tokens_dev, channels)
        x_ref[low:high] = x_ref[low:high] + mm(belong, tall_rows)

    whole(HALF, 0)
    whole(HALF + 1, 1)

    def decoded(part, first, size, rows):
        out_ref[0, first : first + size] = rows.astype(BF16)

    last(HALF + 2, 1, decoded)

    for sides in (mask_sides, range_sides, range_far, atom_sides, bias_sides, row_sides, row_far, *enc_sides):
        sides.sent()
    if depth == 3:
        z_copy(order(2)).wait_send()
    elif depth > 3:
        pl.when(inside)(lambda: z_copy(order(2)).wait_send())
    for step in range(depth):
        if step > 2:
            z_copy(order(step)).wait_send()
        y_copy(step).wait_send()
        c_copy(step, 0).wait_send()
        c_copy(step, 1).wait_send()


def shards(
    count,
    atoms,
    s_cond,
    token_start,
    token_len,
    atom_mask,
    atom_bias,
    pair_bias,
    atom_proj,
    atom_up,
    atom_down,
    atom_gains,
    to_token,
    token_proj,
    token_gain,
    to_atom,
):
    atoms_dev, channels = atoms.shape[1:]
    tokens_dev, width = s_cond.shape
    layers = 2 * HALF
    vmem = pl.BlockSpec(memory_space=pltpu.VMEM)
    hbm = pl.BlockSpec(memory_space=pl.ANY)
    half = HT // 2
    depth = count // 4
    spread = atoms_dev + 2 * PAD
    return pl.pallas_call(
        functools.partial(kernel, count),
        out_shape=pltpu.VMEM(atoms.shape, BF16),
        in_specs=[hbm, hbm, vmem, vmem, vmem] + [hbm] * 5 + [vmem, hbm, hbm, vmem, hbm],
        out_specs=vmem,
        scratch_shapes=[
            pltpu.VMEM((spread, channels), BF16),
            pltpu.VMEM((spread, channels), F32),
            pltpu.VMEM((2, spread, channels), BF16),
            pltpu.VMEM((spread, channels), BF16),
            pltpu.VMEM((spread, channels), BF16),
            pltpu.VMEM((HA, atoms_dev + 2 * EDGE, WK), F32),
            pltpu.VMEM((2, HA, EDGE - WQ + RIM % WQ, WK), BF16),
            pltpu.VMEM((2, HA, EDGE, WK), BF16),
            pltpu.VMEM(pair_bias.shape, BF16),
            pltpu.VMEM((layers, channels, 3 * channels), BF16),
            pltpu.VMEM((layers, channels, channels), BF16),
            pltpu.VMEM(atom_up.shape, BF16),
            pltpu.VMEM(atom_down.shape, BF16),
            pltpu.VMEM(to_token.shape, BF16),
            pltpu.VMEM(to_atom.shape, BF16),
            pltpu.VMEM(s_cond.shape, BF16),
            pltpu.VMEM(token_proj.shape, BF16),
            pltpu.VMEM((3, atoms_dev // LANES, LANES), jnp.int32),
            pltpu.VMEM((atoms_dev // WQ + 2 * SPARE[0], HA * WQ, WK), BF16),
            pltpu.VMEM((5, 8, pl.cdiv(tokens_dev, LANES) * LANES), jnp.int32),
            pltpu.VMEM((3, atoms_dev, channels), BF16),
            pltpu.VMEM((5, tokens_dev, channels), BF16),
            pltpu.VMEM((count, tokens_dev, width), BF16),
            pltpu.VMEM((tokens_dev, width), F32),
            pltpu.VMEM((HT * tokens_dev, width), BF16),
            pltpu.VMEM((2, half * tokens_dev, width // 2 + LANES), F32),
            pltpu.VMEM((HT * tokens_dev, LANES), F32),
            pltpu.SemaphoreType.DMA((13,)),
            pltpu.SemaphoreType.DMA((7, 2)),
            pltpu.SemaphoreType.DMA((7, 2)),
            pltpu.SemaphoreType.DMA((2, 2)),
            pltpu.SemaphoreType.DMA((2, 2)),
            pltpu.SemaphoreType.DMA((depth,)),
            pltpu.SemaphoreType.DMA((depth,)),
            pltpu.SemaphoreType.DMA((2, depth)),
            pltpu.SemaphoreType.DMA((count,)),
        ],
        compiler_params=pltpu.CompilerParams(
            collective_id=0, has_side_effects=True, vmem_limit_bytes=60 * 1024 * 1024
        ),
    )(
        atoms,
        s_cond,
        token_start,
        token_len,
        atom_mask,
        atom_bias,
        pair_bias,
        atom_proj,
        atom_up,
        atom_down,
        atom_gains,
        to_token,
        token_proj,
        token_gain,
        to_atom,
    )


def solution(mesh):
    placed = (
        P("groups", "seq", None),
        P(("groups", "seq"), None),
        P(("groups", "seq")),
        P(("groups", "seq")),
        P(("groups", "seq")),
        P("groups", "seq", None),
        P("groups", "seq", None),
        P(),
        P(),
        P(),
        P(),
        P(),
        P(),
        P(),
        P(),
    )
    return jax.shard_map(
        functools.partial(shards, mesh.shape["seq"]),
        mesh=mesh,
        in_specs=placed,
        out_specs=P("groups", "seq", None),
        check_vma=False,
    )
```

```python
import functools

import jax
import jax.numpy as jnp
from jax import lax
from jax.experimental import pallas as pl
from jax.experimental.pallas import tpu as pltpu
from jax.sharding import PartitionSpec as P

HT = 16
HA = 4
WQ = 32
WK = 128
HALF = 3
TEAMS = 4
U_PARTS = 2
RIM = (WK - WQ) // 2
LANES = 128
SPARE = (4, 2, 0)
EDGE = SPARE[0] * WQ
PAD = EDGE + RIM
KEPT = (SPARE[1] * WQ + RIM, RIM, 0)

epsilon = 1e-05
masked = -1000000000.0
LOG2E = 1.4426950408889634
MESH = pl.DeviceIdType.MESH
F32 = jnp.float32
BF16 = jnp.bfloat16

MASK, RANGE, ATOMS, BIAS, ENC, ROWS = 0, 1, 2, 3, 4, 6
ENC_SHARE = (5, 3)
ENC_PARTS = len(ENC_SHARE)
NORM_ROWS, GATE_ROWS = 64, 32
REACH = (-1, 1, -2, 2)


def layer_norm(values, gain_vec):
    average = jnp.mean(values, axis=-1, keepdims=True)
    centred = values - average
    spread = jnp.mean(centred * centred, axis=-1, keepdims=True)
    return centred * lax.rsqrt(spread + epsilon) * gain_vec


def mm(left, right):
    return jnp.dot(left, right, preferred_element_type=F32)


def mm_nt(left, right):
    return lax.dot_general(left, right, (((1,), (1,)), ((), ())), preferred_element_type=F32)


def head_mask(rows, row_size, cols, col_size):
    row_head = lax.broadcasted_iota(jnp.int32, (rows, cols), 0) // row_size
    col_head = lax.broadcasted_iota(jnp.int32, (rows, cols), 1) // col_size
    return row_head == col_head


def pieces(low, high, most):
    units = (high - low) // 16
    number = pl.cdiv(high - low, most)
    marks = [low + 16 * (units * i // number) for i in range(number)] + [high]
    return list(zip(marks[:-1], marks[1:]))


def kernel(
    count,
    atoms_hbm,
    s_cond_hbm,
    start_hbm,
    length_hbm,
    mask_hbm,
    bias_hbm,
    pair_hbm,
    proj_hbm,
    up_hbm,
    down_hbm,
    gains_hbm,
    to_token_hbm,
    token_proj_hbm,
    token_gain_hbm,
    to_atom_hbm,
    out_ref,
    start_ref,
    length_ref,
    mask_ref,
    gains_ref,
    token_gain_ref,
    atx_ref,
    x_ref,
    kv_ref,
    q_ref,
    mix_ref,
    h_ref,
    gate_ref,
    hidden_ref,
    bias_ref,
    shift_ref,
    beyond_ref,
    pair_ref,
    qkv_w,
    o_w,
    up_ref,
    down_ref,
    to_token_ref,
    to_atom_ref,
    s_cond_ref,
    tp_ref,
    mex_ref,
    wt_ref,
    rngx_ref,
    encx_ref,
    rowsx_ref,
    uall_ref,
    feat_ref,
    qk_ref,
    acc_ref,
    max_ref,
    load_sem,
    side_send,
    side_recv,
    far_send,
    far_recv,
    z_send,
    y_send,
    c_send,
    u_recv,
):
    me = lax.axis_index("seq")
    core = lax.rem(me, 2)
    row_y = lax.rem(me // 2, 2)
    row_z = me // 4
    depth = count // 4
    atoms_dev = atoms_hbm.shape[1]
    channels = atoms_hbm.shape[2]
    tokens_dev, width = s_cond_ref.shape
    windows = atoms_dev // WQ
    head_size = channels // HA
    token_head = width // HT
    core_peer = me + 1 - 2 * core
    y_peer = me + 2 - 4 * row_y
    own = slice(PAD, PAD + atoms_dev)
    bias_rows = EDGE - WQ + RIM % WQ

    def there(offset):
        return me + offset >= 0 if offset < 0 else me + offset < count

    def load(index, source, target):
        copy = pltpu.make_async_copy(source, target, load_sem.at[index])
        copy.start()
        return copy

    gains_load = load(14, gains_hbm, gains_ref)
    atoms_load = load(0, atoms_hbm.at[0], atx_ref.at[pl.ds(PAD, atoms_dev)])
    qkv_loads = [
        load(1 + k, proj_hbm.at[:, k], qkv_w.at[:, :, pl.ds(k * channels, channels)]) for k in range(3)
    ]
    bias_load = load(4, bias_hbm, bias_ref.at[:, pl.ds(EDGE, atoms_dev)])
    small_loads = [
        load(15, mask_hbm, mask_ref),
        load(16, start_hbm, start_ref),
        load(17, length_hbm, length_ref),
    ]

    barrier = pltpu.get_barrier_semaphore()

    def greet(target):
        pl.semaphore_signal(barrier, inc=1, device_id={"seq": target}, device_id_type=MESH)

    for offset in REACH:
        pl.when(there(offset))(lambda: greet(me + offset))
    for z in range(depth):
        pl.when(row_z != z)(lambda: greet(me + 4 * (z - row_z)))

    o_load = load(5, proj_hbm.at[:, 3], o_w)
    hidden_units = up_hbm.shape[3]
    up_loads = [
        load(6 + 7 * k, up_hbm.at[:, k], up_ref.at[:, :, pl.ds(k * hidden_units, hidden_units)]) for k in range(2)
    ]
    down_load = load(7, down_hbm, down_ref)
    pool_loads = [load(8, to_token_hbm, to_token_ref), load(9, s_cond_hbm, s_cond_ref)]
    tp_load = load(10, token_proj_hbm, tp_ref)
    pair_load = load(11, pair_hbm, pair_ref)
    to_atom_load = load(12, to_atom_hbm, to_atom_ref)
    token_gain_load = load(18, token_gain_hbm, token_gain_ref)


    def zero(ref, slot):
        ref[slot] = jnp.zeros(ref.shape[1:], ref.dtype)

    def clear_near(side):
        for ref in (mex_ref, encx_ref):
            zero(ref, 2 * side)
        for ref in (rngx_ref, rowsx_ref):
            zero(ref, 1 + 2 * side)
        rows = slice(0, PAD) if side == 0 else slice(PAD + atoms_dev, 2 * PAD + atoms_dev)
        atx_ref[rows] = jnp.zeros((PAD, channels), BF16)
        zero(beyond_ref, side)

    def clear_far(side):
        for ref in (rngx_ref, rowsx_ref):
            zero(ref, 4 * side)

    for side in range(2):
        sign = 2 * side - 1
        pl.when(jnp.logical_not(there(sign)))(lambda: clear_near(side))
        pl.when(jnp.logical_not(there(2 * sign)))(lambda: clear_far(side))
    beyond_ref[0, :, 0 : EDGE - bias_rows] = jnp.zeros((HA, EDGE - bias_rows, WK), BF16)
    beyond_ref[1, :, bias_rows:] = jnp.zeros((HA, EDGE - bias_rows, WK), BF16)

    class Sides:
        def __init__(self, reach, send, recv, to_left, to_right):
            self.reach = reach
            self.copies = [
                pltpu.make_async_remote_copy(
                    source, target, send(i), recv(i), device_id={"seq": me + sign * reach}, device_id_type=MESH
                )
                for i, (sign, (source, target)) in enumerate(zip((-1, 1), (to_left, to_right)))
            ]

        def start(self):
            pl.when(there(-self.reach))(lambda: self.copies[0].start())
            pl.when(there(self.reach))(lambda: self.copies[1].start())

        def receive(self):
            pl.when(there(self.reach))(lambda: self.copies[0].wait_recv())
            pl.when(there(-self.reach))(lambda: self.copies[1].wait_recv())

        def sent(self):
            pl.when(there(-self.reach))(lambda: self.copies[0].wait_send())
            pl.when(there(self.reach))(lambda: self.copies[1].wait_send())

    def near(kind, to_left, to_right):
        return Sides(1, lambda i: side_send.at[kind, i], lambda i: side_recv.at[kind, i], to_left, to_right)

    def far(kind, to_left, to_right):
        return Sides(2, lambda i: far_send.at[kind, i], lambda i: far_recv.at[kind, i], to_left, to_right)

    mask_sides = near(MASK, (mex_ref.at[1], mex_ref.at[2]), (mex_ref.at[1], mex_ref.at[0]))
    range_sides = near(RANGE, (rngx_ref.at[2], rngx_ref.at[3]), (rngx_ref.at[2], rngx_ref.at[1]))
    range_far = far(0, (rngx_ref.at[2], rngx_ref.at[4]), (rngx_ref.at[2], rngx_ref.at[0]))
    row_sides = near(ROWS, (rowsx_ref.at[2], rowsx_ref.at[3]), (rowsx_ref.at[2], rowsx_ref.at[1]))
    row_far = far(1, (rowsx_ref.at[2], rowsx_ref.at[4]), (rowsx_ref.at[2], rowsx_ref.at[0]))
    atom_sides = near(
        ATOMS,
        (atoms_hbm.at[0, pl.ds(0, PAD)], atx_ref.at[pl.ds(PAD + atoms_dev, PAD)]),
        (atoms_hbm.at[0, pl.ds(atoms_dev - PAD, PAD)], atx_ref.at[pl.ds(0, PAD)]),
    )
    bias_sides = near(
        BIAS,
        (shift_ref.at[0], beyond_ref.at[1, :, pl.ds(0, bias_rows)]),
        (shift_ref.at[1], beyond_ref.at[0, :, pl.ds(EDGE - bias_rows, bias_rows)]),
    )
    enc_marks = [windows * sum(ENC_SHARE[:part]) // sum(ENC_SHARE) for part in range(ENC_PARTS + 1)]
    enc_rows = [(WQ * a, WQ * b) for a, b in zip(enc_marks[:-1], enc_marks[1:])]

    def enc_part(part):
        rows = pl.ds(enc_rows[part][0], enc_rows[part][1] - enc_rows[part][0])
        return near(
            ENC + part,
            (encx_ref.at[1, rows], encx_ref.at[2, rows]),
            (encx_ref.at[1, rows], encx_ref.at[0, rows]),
        )

    enc_sides = [enc_part(part) for part in range(ENC_PARTS)]

    mask_lines = atoms_dev // LANES

    def mask_row(index):
        return mex_ref[index // mask_lines, index % mask_lines : index % mask_lines + 1, :]

    def window_mask(window):
        first = atoms_dev + window * WQ - RIM
        row, offset = first // LANES, first % LANES
        line = mask_row(row)
        if offset:
            line = jnp.concatenate([line[:, offset:], mask_row(row + 1)[:, :offset]], axis=1)
        return jnp.where(line == 1, 0.0, masked).astype(F32)

    atom_heads = head_mask(HA * WQ, WQ, channels, head_size)


    both_heads = jnp.concatenate([atom_heads] * 2, axis=1)

    def score(layer, window, fresh):
        first = PAD + window * WQ
        query = q_ref[layer % 2, first : first + WQ, :]
        tall = jnp.where(atom_heads, jnp.concatenate([query] * HA, axis=0), jnp.zeros((), BF16))
        keys = kv_ref[layer % 2, 0, first - RIM : first - RIM + WK, :]
        rows = slice(EDGE + window * WQ, EDGE + window * WQ + WQ)
        if fresh and not 0 <= window < windows:
            side, near_row = (0, EDGE + window * WQ) if window < 0 else (1, window * WQ - atoms_dev)
            bias = beyond_ref[side, :, near_row : near_row + WQ, :].astype(F32)
            bias = bias + window_mask(window) * LOG2E
            bias_ref[:, rows, :] = bias
        elif fresh:
            bias = (bias_ref[:, rows, :] + window_mask(window)) * LOG2E
            bias_ref[:, rows, :] = bias
        else:
            bias = bias_ref[:, rows, :]
        return mm_nt(tall, keys) + bias.reshape(HA * WQ, WK)

    def soft(logits):
        return jnp.exp2(logits - jnp.max(logits, axis=-1, keepdims=True)).astype(BF16)

    def mix(layer, window, weights):
        first = PAD + window * WQ
        values = jnp.concatenate(
            [kv_ref[layer % 2, 1, first - RIM : first - RIM + WK, :], jnp.ones((WK, channels), BF16)], axis=1
        )
        both = jnp.where(both_heads, mm(weights, values), 0.0)
        joined = both[0:WQ]
        for head in range(1, HA):
            joined = joined + both[head * WQ : (head + 1) * WQ]
        mix_ref[first : first + WQ, :] = (joined[:, :channels] / joined[:, channels:]).astype(BF16)

    def attend_steps(layer, which, fresh=False):
        def one(window):
            wt_ref[window + SPARE[0]] = soft(score(layer, window, fresh))

        return [functools.partial(one, window) for window in which] + [
            lambda window=window: mix(layer, window, wt_ref[window + SPARE[0]]) for window in which
        ]

    def attend_all(layer, which, fresh=False):
        together(attend_steps(layer, which, fresh))

    def together(*works):
        steps = [((i + 0.5) / len(work), k, step) for k, work in enumerate(works) for i, step in enumerate(work)]
        for _, _, step in sorted(steps, key=lambda entry: entry[:2]):
            step()

    def rows_of(ref, ranges):
        parts = [ref[a:b] for a, b in ranges]
        return parts[0] if len(parts) == 1 else jnp.concatenate(parts, axis=0)

    def write_rows(ref, ranges, values):
        first = 0
        for a, b in ranges:
            ref[a:b] = values[first : first + b - a]
            first += b - a

    def bits(ranges, most):
        return [piece for a, b in ranges for piece in pieces(a, b, most)]

    def norm(layer, which, ranges):
        gain = gains_ref[layer, which : which + 1]
        for a, b in bits(ranges, NORM_ROWS):
            h_ref[a:b] = layer_norm(x_ref[a:b], gain).astype(BF16)

    def project(layer, ranges):
        side = layer % 2
        norm(layer, 0, ranges)
        out = mm(rows_of(h_ref, ranges), qkv_w[layer])
        write_rows(q_ref.at[side], ranges, (out[:, :channels] * (LOG2E * head_size ** (-0.5))).astype(BF16))
        for kind in range(2):
            write_rows(
                kv_ref.at[side, kind], ranges, out[:, (kind + 1) * channels : (kind + 2) * channels].astype(BF16)
            )

    def transition_steps(layer, ranges, keep):
        hidden = gate_ref.shape[1] // 2

        def attach():
            write_rows(x_ref, ranges, rows_of(x_ref, ranges) + mm(rows_of(mix_ref, ranges), o_w[layer]))

        def spread_out():
            write_rows(gate_ref, ranges, mm(rows_of(h_ref, ranges), up_ref[layer]))

        def gated(a, b):
            gate = 0.5 * gate_ref[a:b, :hidden]
            product = (gate + gate * jnp.tanh(gate)) * gate_ref[a:b, hidden:]
            hidden_ref[a:b] = product.astype(BF16)

        def finish():
            keep(ranges, rows_of(x_ref, ranges) + mm(rows_of(hidden_ref, ranges), down_ref[layer]))

        steps = [attach, lambda: norm(layer, 1, ranges), spread_out]
        steps += [functools.partial(gated, a, b) for a, b in bits(ranges, GATE_ROWS)]
        return steps + [finish]

    def transition(layer, ranges, keep):
        together(transition_steps(layer, ranges, keep))

    def keep_x(ranges, rows):
        write_rows(x_ref, ranges, rows)

    def advance(layer, ranges):
        transition(layer, ranges, keep_x)
        project(layer + 1, ranges)

    def outside(layer):
        side = layer % 2

        def clear_rows(first):
            for kind in range(2):
                kv_ref[side, kind, first : first + PAD] = jnp.zeros((PAD, channels), BF16)

        pl.when(jnp.logical_not(there(-1)))(lambda: clear_rows(0))
        pl.when(jnp.logical_not(there(1)))(lambda: clear_rows(PAD + atoms_dev))

    def whole(layer, step):
        spare, kept = SPARE[step], KEPT[step]
        attend_all(layer, range(-spare, windows + spare))
        advance(layer, [(PAD - kept, PAD + atoms_dev + kept)])
        outside(layer + 1)

    gains_load.wait()
    atoms_load.wait()
    for copy in qkv_loads:
        copy.wait()
    x_ref[own] = atx_ref[own].astype(F32)
    project(0, [(PAD, PAD + atoms_dev)])

    for copy in small_loads:
        copy.wait()
    mex_ref[1] = mask_ref[...].reshape(mex_ref.shape[1:])
    starts = start_ref[...].reshape(1, tokens_dev)
    rngx_ref[2, 0:1, 0:tokens_dev] = starts
    rngx_ref[2, 1:2, 0:tokens_dev] = starts + length_ref[...].reshape(1, tokens_dev)
    bias_load.wait()
    for side, first in enumerate((EDGE, EDGE + atoms_dev - bias_rows)):
        rows = bias_ref[:, first : first + bias_rows, :]
        largest = jnp.max(rows, axis=-1, keepdims=True)
        shift_ref[side] = ((rows - largest) * LOG2E).astype(BF16)
    peers = (depth - 1) + sum(jnp.where(there(offset), 1, 0) for offset in REACH)
    pl.semaphore_wait(barrier, peers)
    for sides in (mask_sides, atom_sides, bias_sides, range_sides, range_far):
        sides.start()
    inner = range(RIM // WQ + 1, windows - RIM // WQ - 1)
    attend_all(0, inner, fresh=True)
    o_load.wait()
    for copy in up_loads:
        copy.wait()
    down_load.wait()
    begin, end = PAD + inner[0] * WQ, PAD + (inner[-1] + 1) * WQ
    advance(0, [(begin, end)])
    mask_sides.receive()
    atom_sides.receive()
    beside = ((0, PAD), (PAD + atoms_dev, 2 * PAD + atoms_dev))
    for a, b in beside:
        x_ref[a:b] = atx_ref[a:b].astype(F32)
    project(0, beside)
    attend_all(0, [w for w in range(windows) if w not in inner], fresh=True)
    bias_sides.receive()
    attend_all(0, [w for w in range(-SPARE[0], windows + SPARE[0]) if w < 0 or w >= windows], fresh=True)
    advance(0, [(PAD - KEPT[0], begin), (end, PAD + atoms_dev + KEPT[0])])
    outside(1)
    whole(1, 1)

    def keep_encoded(group, rows):
        keep_x(group, rows)
        write_rows(encx_ref.at[1], [(a - PAD, b - PAD) for a, b in group], rows.astype(BF16))

    attend_all(2, range(*enc_marks[0:2]))
    for part in range(ENC_PARTS):
        a, b = enc_rows[part]
        work = transition_steps(2, [(PAD + a, PAD + b)], keep_encoded)
        if part + 1 < ENC_PARTS:
            together(attend_steps(2, range(*enc_marks[part + 1 : part + 3])), work)
        else:
            together(work)
        enc_sides[part].start()

    range_sides.receive()
    range_far.receive()
    for copy in pool_loads:
        copy.wait()
    token_gain_load.wait()
    eye = head_mask(tokens_dev, 1, tokens_dev, 1)

    def column(line):
        return jnp.sum(jnp.where(eye, line.astype(F32), 0.0), axis=1, keepdims=True)

    start_col = column(rngx_ref[2, 0:1, 0:tokens_dev])
    end_col = column(rngx_ref[2, 1:2, 0:tokens_dev])

    def pooled(blocks, low, high):
        rows = jnp.concatenate([encx_ref[block, low:high] for block in blocks], axis=0)
        projected = jnp.maximum(mm(rows, to_token_ref[...]), 0.0).astype(BF16)
        place = jnp.concatenate(
            [
                (me + block - 1) * atoms_dev
                + low
                + lax.broadcasted_iota(jnp.int32, (tokens_dev, high - low), 1)
                for block in blocks
            ],
            axis=1,
        ).astype(F32)
        member = jnp.where((place >= start_col) & (place < end_col), 1.0, 0.0).astype(BF16)
        return mm(member, projected)

    totals = pooled((1,), 0, atoms_dev)
    for part in range(ENC_PARTS):
        enc_sides[part].receive()
        totals = totals + pooled((0, 2), *enc_rows[part])
    features = totals / (end_col - start_col) + s_cond_ref[...].astype(F32)
    feat_ref[...] = features
    uall_ref[me] = layer_norm(features, token_gain_ref[...].reshape(1, width)).astype(BF16)

    def at(z, y, c):
        return (z * 2 + y) * 2 + c

    u_rows = tokens_dev // U_PARTS

    def u_copy(index, part, target, send):
        rows = uall_ref.at[index, pl.ds(part * u_rows, u_rows)]
        return pltpu.make_async_remote_copy(
            rows, rows, send, u_recv.at[index, part], device_id={"seq": target}, device_id_type=MESH
        )

    def u_arrived(index, part):
        u_copy(index, part, core_peer, c_send.at[0, 0, part]).wait_recv()

    def z_copy(z, part):
        return u_copy(me, part, at(z, row_y, core), z_send.at[z, part])

    def y_copy(z, part):
        return u_copy(at(z, row_y, core), part, y_peer, y_send.at[z, part])

    def c_copy(z, kind, part):
        return u_copy(at(z, (row_y + kind) % 2, core), part, core_peer, c_send.at[kind, z, part])

    def start(copy, *place):
        for part in range(U_PARTS):
            copy(*place, part).start()

    def sent(copy, *place):
        for part in range(U_PARTS):
            copy(*place, part).wait_send()

    shorter = jnp.minimum(row_z, depth - 1 - row_z)
    upward = jnp.where(depth - 1 - row_z > row_z, 1, -1)

    def order(step):
        turn = jnp.where(step % 2 == 1, (step + 1) // 2, -(step // 2))
        return row_z + jnp.where(step <= 2 * shorter, turn, upward * (step - shorter))

    def near_sends(step):
        start(z_copy, order(step))

    at_end = shorter == 0
    inside = jnp.logical_not(at_end)
    start(y_copy, row_z)
    if depth > 1:
        near_sends(1)
    if depth > 2:
        pl.when(inside)(lambda: near_sends(2))
    start(c_copy, row_z, 0)

    def relay(z):
        for part in range(U_PARTS):
            u_arrived(at(z, row_y, core), part)
            y_copy(z, part).start()
            c_copy(z, 0, part).start()

    def across(z):
        for part in range(U_PARTS):
            u_arrived(at(z, 1 - row_y, core), part)
            c_copy(z, 1, part).start()

    tp_load.wait()
    team = HT // TEAMS
    team_rows, team_width = team * tokens_dev, width // TEAMS
    token_heads = head_mask(team_rows, tokens_dev, team_width, token_head)
    query = mm(uall_ref[me], tp_ref[0]).astype(BF16)
    for part in range(TEAMS):
        cols = slice(part * team_width, (part + 1) * team_width)
        apart = jnp.where(
            token_heads, jnp.concatenate([query[:, cols]] * team, axis=0), jnp.zeros((), BF16)
        )
        folded = mm_nt(apart, tp_ref[1, :, cols]) * token_head ** (-0.5)
        qk_ref[part * team_rows : (part + 1) * team_rows] = folded.astype(BF16)
    max_ref[...] = jnp.full_like(max_ref, -1e30)
    acc_ref[...] = jnp.zeros_like(acc_ref)
    pair_load.wait()
    span = 4 * tokens_dev

    def token_block(places):
        rows = jnp.concatenate(
            [uall_ref[pl.ds(at(z, y, 0), 2)].reshape(2 * tokens_dev, width) for z, y in places], axis=0
        )
        bias = jnp.concatenate(
            [
                pair_ref[:, :, pl.ds(pl.multiple_of(at(z, y, 0) * tokens_dev, 2 * tokens_dev), 2 * tokens_dev)]
                for z, y in places
            ],
            axis=2,
        )
        bias = bias.reshape(HT * tokens_dev, span).astype(F32)
        logits = mm_nt(qk_ref[...], rows) + bias
        before = max_ref[...]
        now = jnp.maximum(before, jnp.max(logits, axis=-1, keepdims=True))
        max_ref[...] = now
        weights = jnp.exp(logits - jnp.concatenate([now] * (span // LANES), axis=1)).astype(BF16)
        shrink = jnp.exp(before - now)
        values = mm(rows, tp_ref[2]).astype(BF16)
        for part in range(TEAMS):
            lines = slice(part * team_rows, (part + 1) * team_rows)
            ones = jnp.ones((span, acc_ref.shape[1] - team_width), BF16)
            beside = jnp.concatenate([values[:, part * team_width : (part + 1) * team_width], ones], axis=1)
            scale = jnp.concatenate([shrink[lines]] * (acc_ref.shape[1] // LANES), axis=1)
            acc_ref[lines] = acc_ref[lines] * scale + mm(weights[lines], beside)

    if depth > 1:
        sent(z_copy, order(1))
    if depth > 2:
        pl.when(at_end)(lambda: near_sends(2))
    if depth > 3:
        pl.when(inside)(lambda: near_sends(3))
    across(order(0))
    if depth > 1:
        relay(order(1))

    def far_sends():
        sent(z_copy, order(2))
        near_sends(3)

    if depth > 3:
        pl.when(at_end)(far_sends)
    for step in range(4, depth):
        near_sends(step)

    def other_core(step, kind):
        for part in range(U_PARTS):
            u_arrived(at(order(step), (row_y + kind) % 2, 1 - core), part)

    def token_pairs(step, kind):
        token_block([(order(step + i), (row_y + kind) % 2) for i in range(2)])

    def token_step(turn, carry):
        step = 2 * turn
        other_core(step, 0)
        other_core(step + 1, 0)
        token_pairs(step, 0)
        pl.when(step + 2 < depth)(lambda: relay(order(step + 2)))
        across(order(step + 1))
        pl.when(step + 3 < depth)(lambda: relay(order(step + 3)))
        other_core(step, 1)
        other_core(step + 1, 1)
        token_pairs(step, 1)
        pl.when(step + 2 < depth)(lambda: across(order(step + 2)))
        return carry

    lax.fori_loop(0, depth // 2, token_step, 0)

    parts = []
    for part in range(TEAMS):
        lines = slice(part * team_rows, (part + 1) * team_rows)
        mixed = acc_ref[lines, 0:team_width] * (1.0 / acc_ref[lines, team_width : team_width + 1])
        mixed = jnp.where(token_heads, mixed, 0.0)
        joined = mixed[0:tokens_dev]
        for head in range(1, team):
            joined = joined + mixed[head * tokens_dev : (head + 1) * tokens_dev]
        parts.append(joined.astype(BF16))
    token_mix = jnp.concatenate(parts, axis=1)
    updated = feat_ref[...] + mm(token_mix, tp_ref[3])
    to_atom_load.wait()
    rowsx_ref[2] = mm(updated.astype(BF16), to_atom_ref[...]).astype(BF16)
    row_sides.start()
    row_far.start()

    areas = ((0, PAD, 0), (PAD, PAD + atoms_dev, 1), (PAD + atoms_dev, 2 * PAD + atoms_dev, 2))

    def members(low, high, slot):
        shape = (high - low, 3 * tokens_dev)
        place = me * atoms_dev + low - PAD + lax.broadcasted_iota(jnp.int32, shape, 0)
        place = place.astype(F32)
        first, end = (
            jnp.concatenate([rngx_ref[slot + i, k : k + 1, 0:tokens_dev] for i in range(3)], axis=1).astype(F32)
            for k in range(2)
        )
        return jnp.where((place >= first) & (place < end), 1.0, 0.0).astype(BF16)

    x_ref[0:PAD] = encx_ref[0, atoms_dev - PAD : atoms_dev].astype(F32)
    x_ref[PAD + atoms_dev :] = encx_ref[2, 0:PAD].astype(F32)
    belongs = [members(*area) for area in areas]
    row_sides.receive()
    row_far.receive()
    for belong, (low, high, slot) in zip(belongs, areas):
        tall_rows = rowsx_ref[slot : slot + 3].reshape(3 * tokens_dev, channels)
        x_ref[low:high] = x_ref[low:high] + mm(belong, tall_rows)

    project(HALF, [(0, atoms_dev + 2 * PAD)])
    outside(HALF)
    whole(HALF, 0)
    whole(HALF + 1, 1)

    def keep_decoded(group, rows):
        for a, b in group:
            out_ref[0, a - PAD : b - PAD] = rows.astype(BF16)

    attend_all(HALF + 2, range(windows))
    transition(HALF + 2, [(PAD, PAD + atoms_dev)], keep_decoded)

    for sides in (mask_sides, range_sides, range_far, atom_sides, bias_sides, row_sides, row_far, *enc_sides):
        sides.sent()
    if depth == 3:
        sent(z_copy, order(2))
    elif depth > 3:
        pl.when(inside)(lambda: sent(z_copy, order(2)))
    for step in range(depth):
        if step > 2:
            sent(z_copy, order(step))
        sent(y_copy, step)
        sent(c_copy, step, 0)
        sent(c_copy, step, 1)


def shards(
    count,
    atoms,
    s_cond,
    token_start,
    token_len,
    atom_mask,
    atom_bias,
    pair_bias,
    atom_proj,
    atom_up,
    atom_down,
    atom_gains,
    to_token,
    token_proj,
    token_gain,
    to_atom,
):
    atoms_dev, channels = atoms.shape[1:]
    tokens_dev, width = s_cond.shape
    layers = 2 * HALF
    vmem = pl.BlockSpec(memory_space=pltpu.VMEM)
    hbm = pl.BlockSpec(memory_space=pl.ANY)
    depth = count // 4
    spread = atoms_dev + 2 * PAD
    return pl.pallas_call(
        functools.partial(kernel, count),
        out_shape=pltpu.VMEM(atoms.shape, BF16),
        in_specs=[hbm] * 15,
        out_specs=vmem,
        scratch_shapes=[
            pltpu.VMEM(token_start.shape, jnp.int32),
            pltpu.VMEM(token_len.shape, jnp.int32),
            pltpu.VMEM(atom_mask.shape, jnp.int32),
            pltpu.VMEM(atom_gains.shape, F32),
            pltpu.VMEM(token_gain.shape, F32),
            pltpu.VMEM((spread, channels), BF16),
            pltpu.VMEM((spread, channels), F32),
            pltpu.VMEM((2, 2, spread, channels), BF16),
            pltpu.VMEM((2, spread, channels), BF16),
            pltpu.VMEM((spread, channels), BF16),
            pltpu.VMEM((spread, channels), BF16),
            pltpu.VMEM((spread, 2 * atom_up.shape[3]), F32),
            pltpu.VMEM((spread, atom_up.shape[3]), BF16),
            pltpu.VMEM((HA, atoms_dev + 2 * EDGE, WK), F32),
            pltpu.VMEM((2, HA, EDGE - WQ + RIM % WQ, WK), BF16),
            pltpu.VMEM((2, HA, EDGE, WK), BF16),
            pltpu.VMEM(pair_bias.shape, BF16),
            pltpu.VMEM((layers, channels, 3 * channels), BF16),
            pltpu.VMEM((layers, channels, channels), BF16),
            pltpu.VMEM((layers, channels, 2 * atom_up.shape[3]), BF16),
            pltpu.VMEM(atom_down.shape, BF16),
            pltpu.VMEM(to_token.shape, BF16),
            pltpu.VMEM(to_atom.shape, BF16),
            pltpu.VMEM(s_cond.shape, BF16),
            pltpu.VMEM(token_proj.shape, BF16),
            pltpu.VMEM((3, atoms_dev // LANES, LANES), jnp.int32),
            pltpu.VMEM((atoms_dev // WQ + 2 * SPARE[0], HA * WQ, WK), BF16),
            pltpu.VMEM((5, 8, pl.cdiv(tokens_dev, LANES) * LANES), jnp.int32),
            pltpu.VMEM((3, atoms_dev, channels), BF16),
            pltpu.VMEM((5, tokens_dev, channels), BF16),
            pltpu.VMEM((count, tokens_dev, width), BF16),
            pltpu.VMEM((tokens_dev, width), F32),
            pltpu.VMEM((HT * tokens_dev, width), BF16),
            pltpu.VMEM((HT * tokens_dev, pl.cdiv(width // TEAMS + 1, LANES) * LANES), F32),
            pltpu.VMEM((HT * tokens_dev, LANES), F32),
            pltpu.SemaphoreType.DMA((19,)),
            pltpu.SemaphoreType.DMA((7, 2)),
            pltpu.SemaphoreType.DMA((7, 2)),
            pltpu.SemaphoreType.DMA((2, 2)),
            pltpu.SemaphoreType.DMA((2, 2)),
            pltpu.SemaphoreType.DMA((depth, U_PARTS)),
            pltpu.SemaphoreType.DMA((depth, U_PARTS)),
            pltpu.SemaphoreType.DMA((2, depth, U_PARTS)),
            pltpu.SemaphoreType.DMA((count, U_PARTS)),
        ],
        compiler_params=pltpu.CompilerParams(
            collective_id=0, has_side_effects=True, vmem_limit_bytes=60 * 1024 * 1024
        ),
    )(
        atoms,
        s_cond,
        token_start,
        token_len,
        atom_mask,
        atom_bias,
        pair_bias,
        atom_proj,
        atom_up,
        atom_down,
        atom_gains,
        to_token,
        token_proj,
        token_gain,
        to_atom,
    )


def solution(mesh):
    placed = (
        P("groups", "seq", None),
        P(("groups", "seq"), None),
        P(("groups", "seq")),
        P(("groups", "seq")),
        P(("groups", "seq")),
        P("groups", "seq", None),
        P("groups", "seq", None),
        P(),
        P(),
        P(),
        P(),
        P(),
        P(),
        P(),
        P(),
    )
    return jax.shard_map(
        functools.partial(shards, mesh.shape["seq"]),
        mesh=mesh,
        in_specs=placed,
        out_specs=P("groups", "seq", None),
        check_vma=False,
    )
```

```python
import functools

import jax
import jax.numpy as jnp
from jax import lax
from jax.experimental import pallas as pl
from jax.experimental.pallas import tpu as pltpu
from jax.sharding import PartitionSpec as P

HT = 16
HA = 4
WQ = 32
WK = 128
HALF = 3
TEAMS = 4
U_PARTS = 2
RIM = (WK - WQ) // 2
LANES = 128
SPARE = (4, 2, 0)
EDGE = SPARE[0] * WQ
PAD = EDGE + RIM
KEPT = (SPARE[1] * WQ + RIM, RIM, 0)

epsilon = 1e-05
masked = -1000000000.0
LOG2E = 1.4426950408889634
MESH = pl.DeviceIdType.MESH
F32 = jnp.float32
BF16 = jnp.bfloat16

MASK, RANGE, ATOMS, BIAS, ENC, ROWS = 0, 1, 2, 3, 4, 6
ENC_SHARE = (5, 3)
ENC_PARTS = len(ENC_SHARE)
NORM_ROWS, GATE_ROWS = 64, 32
REACH = (-1, 1, -2, 2)


def layer_norm(values, gain_vec):
    average = jnp.mean(values, axis=-1, keepdims=True)
    centred = values - average
    spread = jnp.mean(centred * centred, axis=-1, keepdims=True)
    return centred * lax.rsqrt(spread + epsilon) * gain_vec


def row_mean(values):
    high = values.astype(BF16)
    low = (values - high.astype(F32)).astype(BF16)
    size = values.shape[-1]
    return mm(jnp.concatenate([high, low], axis=-1), jnp.ones((2 * size, size), BF16)) * (1.0 / size)


def row_norm(values, gain_vec):
    centred = values - row_mean(values)
    return centred * lax.rsqrt(row_mean(centred * centred) + epsilon) * gain_vec


def mm(left, right):
    return jnp.dot(left, right, preferred_element_type=F32)


def mm_nt(left, right):
    return lax.dot_general(left, right, (((1,), (1,)), ((), ())), preferred_element_type=F32)


def head_mask(rows, row_size, cols, col_size):
    row_head = lax.broadcasted_iota(jnp.int32, (rows, cols), 0) // row_size
    col_head = lax.broadcasted_iota(jnp.int32, (rows, cols), 1) // col_size
    return row_head == col_head


def pieces(low, high, most):
    units = (high - low) // 16
    number = pl.cdiv(high - low, most)
    marks = [low + 16 * (units * i // number) for i in range(number)] + [high]
    return list(zip(marks[:-1], marks[1:]))


def kernel(
    count,
    atoms_hbm,
    s_cond_hbm,
    start_hbm,
    length_hbm,
    mask_hbm,
    bias_hbm,
    pair_hbm,
    proj_hbm,
    up_hbm,
    down_hbm,
    gains_hbm,
    to_token_hbm,
    token_proj_hbm,
    token_gain_hbm,
    to_atom_hbm,
    out_ref,
    start_ref,
    length_ref,
    mask_ref,
    gains_ref,
    token_gain_ref,
    atx_ref,
    x_ref,
    kv_ref,
    q_ref,
    mix_ref,
    h_ref,
    gate_ref,
    hidden_ref,
    bias_ref,
    shift_ref,
    beyond_ref,
    pair_ref,
    qkv_w,
    o_w,
    up_ref,
    down_ref,
    to_token_ref,
    to_atom_ref,
    s_cond_ref,
    tp_ref,
    mex_ref,
    wt_ref,
    rngx_ref,
    encx_ref,
    rowsx_ref,
    uall_ref,
    feat_ref,
    qk_ref,
    acc_ref,
    max_ref,
    load_sem,
    side_send,
    side_recv,
    far_send,
    far_recv,
    z_send,
    y_send,
    c_send,
    u_recv,
):
    me = lax.axis_index("seq")
    core = lax.rem(me, 2)
    row_y = lax.rem(me // 2, 2)
    row_z = me // 4
    depth = count // 4
    atoms_dev = atoms_hbm.shape[1]
    channels = atoms_hbm.shape[2]
    tokens_dev, width = s_cond_ref.shape
    windows = atoms_dev // WQ
    head_size = channels // HA
    token_head = width // HT
    core_peer = me + 1 - 2 * core
    y_peer = me + 2 - 4 * row_y
    own = slice(PAD, PAD + atoms_dev)
    bias_rows = EDGE - WQ + RIM % WQ

    def there(offset):
        return me + offset >= 0 if offset < 0 else me + offset < count

    def load(index, source, target):
        copy = pltpu.make_async_copy(source, target, load_sem.at[index])
        copy.start()
        return copy

    gains_load = load(14, gains_hbm, gains_ref)
    atoms_load = load(0, atoms_hbm.at[0], atx_ref.at[pl.ds(PAD, atoms_dev)])
    qkv_loads = [
        load(1 + k, proj_hbm.at[:, k], qkv_w.at[:, :, pl.ds(k * channels, channels)]) for k in range(3)
    ]
    bias_load = load(4, bias_hbm, bias_ref.at[:, pl.ds(EDGE, atoms_dev)])
    small_loads = [
        load(15, mask_hbm, mask_ref),
        load(16, start_hbm, start_ref),
        load(17, length_hbm, length_ref),
    ]

    barrier = pltpu.get_barrier_semaphore()

    def greet(target):
        pl.semaphore_signal(barrier, inc=1, device_id={"seq": target}, device_id_type=MESH)

    for offset in REACH:
        pl.when(there(offset))(lambda: greet(me + offset))
    for z in range(depth):
        pl.when(row_z != z)(lambda: greet(me + 4 * (z - row_z)))

    o_load = load(5, proj_hbm.at[:, 3], o_w)
    hidden_units = up_hbm.shape[3]
    up_loads = [
        load(6 + 7 * k, up_hbm.at[:, k], up_ref.at[:, :, pl.ds(k * hidden_units, hidden_units)]) for k in range(2)
    ]
    down_load = load(7, down_hbm, down_ref)
    def zero(ref, slot):
        ref[slot] = jnp.zeros(ref.shape[1:], ref.dtype)

    def clear_near(side):
        for ref in (mex_ref, encx_ref):
            zero(ref, 2 * side)
        for ref in (rngx_ref, rowsx_ref):
            zero(ref, 1 + 2 * side)
        rows = slice(0, PAD) if side == 0 else slice(PAD + atoms_dev, 2 * PAD + atoms_dev)
        atx_ref[rows] = jnp.zeros((PAD, channels), BF16)
        zero(beyond_ref, side)

    def clear_far(side):
        for ref in (rngx_ref, rowsx_ref):
            zero(ref, 4 * side)

    for side in range(2):
        sign = 2 * side - 1
        pl.when(jnp.logical_not(there(sign)))(lambda: clear_near(side))
        pl.when(jnp.logical_not(there(2 * sign)))(lambda: clear_far(side))
    beyond_ref[0, :, 0 : EDGE - bias_rows] = jnp.zeros((HA, EDGE - bias_rows, WK), BF16)
    beyond_ref[1, :, bias_rows:] = jnp.zeros((HA, EDGE - bias_rows, WK), BF16)

    class Sides:
        def __init__(self, reach, send, recv, to_left, to_right):
            self.reach = reach
            self.copies = [
                pltpu.make_async_remote_copy(
                    source, target, send(i), recv(i), device_id={"seq": me + sign * reach}, device_id_type=MESH
                )
                for i, (sign, (source, target)) in enumerate(zip((-1, 1), (to_left, to_right)))
            ]

        def start(self):
            pl.when(there(-self.reach))(lambda: self.copies[0].start())
            pl.when(there(self.reach))(lambda: self.copies[1].start())

        def receive(self):
            pl.when(there(self.reach))(lambda: self.copies[0].wait_recv())
            pl.when(there(-self.reach))(lambda: self.copies[1].wait_recv())

        def sent(self):
            pl.when(there(-self.reach))(lambda: self.copies[0].wait_send())
            pl.when(there(self.reach))(lambda: self.copies[1].wait_send())

    def near(kind, to_left, to_right):
        return Sides(1, lambda i: side_send.at[kind, i], lambda i: side_recv.at[kind, i], to_left, to_right)

    def far(kind, to_left, to_right):
        return Sides(2, lambda i: far_send.at[kind, i], lambda i: far_recv.at[kind, i], to_left, to_right)

    mask_sides = near(MASK, (mex_ref.at[1], mex_ref.at[2]), (mex_ref.at[1], mex_ref.at[0]))
    range_sides = near(RANGE, (rngx_ref.at[2], rngx_ref.at[3]), (rngx_ref.at[2], rngx_ref.at[1]))
    range_far = far(0, (rngx_ref.at[2], rngx_ref.at[4]), (rngx_ref.at[2], rngx_ref.at[0]))
    row_sides = near(ROWS, (rowsx_ref.at[2], rowsx_ref.at[3]), (rowsx_ref.at[2], rowsx_ref.at[1]))
    row_far = far(1, (rowsx_ref.at[2], rowsx_ref.at[4]), (rowsx_ref.at[2], rowsx_ref.at[0]))
    atom_sides = near(
        ATOMS,
        (atoms_hbm.at[0, pl.ds(0, PAD)], atx_ref.at[pl.ds(PAD + atoms_dev, PAD)]),
        (atoms_hbm.at[0, pl.ds(atoms_dev - PAD, PAD)], atx_ref.at[pl.ds(0, PAD)]),
    )
    bias_sides = near(
        BIAS,
        (shift_ref.at[0], beyond_ref.at[1, :, pl.ds(0, bias_rows)]),
        (shift_ref.at[1], beyond_ref.at[0, :, pl.ds(EDGE - bias_rows, bias_rows)]),
    )
    enc_marks = [windows * sum(ENC_SHARE[:part]) // sum(ENC_SHARE) for part in range(ENC_PARTS + 1)]
    enc_rows = [(WQ * a, WQ * b) for a, b in zip(enc_marks[:-1], enc_marks[1:])]

    def enc_part(part):
        rows = pl.ds(enc_rows[part][0], enc_rows[part][1] - enc_rows[part][0])
        return near(
            ENC + part,
            (encx_ref.at[1, rows], encx_ref.at[2, rows]),
            (encx_ref.at[1, rows], encx_ref.at[0, rows]),
        )

    enc_sides = [enc_part(part) for part in range(ENC_PARTS)]

    mask_lines = atoms_dev // LANES

    def mask_row(index):
        return mex_ref[index // mask_lines, index % mask_lines : index % mask_lines + 1, :]

    def window_mask(window):
        first = atoms_dev + window * WQ - RIM
        row, offset = first // LANES, first % LANES
        line = mask_row(row)
        if offset:
            line = jnp.concatenate([line[:, offset:], mask_row(row + 1)[:, :offset]], axis=1)
        return jnp.where(line == 1, 0.0, masked).astype(F32)

    atom_heads = head_mask(HA * WQ, WQ, channels, head_size)


    both_heads = jnp.concatenate([atom_heads] * 2, axis=1)

    def score(layer, window, fresh):
        first = PAD + window * WQ
        query = q_ref[layer % 2, first : first + WQ, :]
        tall = jnp.where(atom_heads, jnp.concatenate([query] * HA, axis=0), jnp.zeros((), BF16))
        keys = kv_ref[layer % 2, 0, first - RIM : first - RIM + WK, :]
        rows = slice(EDGE + window * WQ, EDGE + window * WQ + WQ)
        if fresh and not 0 <= window < windows:
            side, near_row = (0, EDGE + window * WQ) if window < 0 else (1, window * WQ - atoms_dev)
            bias = beyond_ref[side, :, near_row : near_row + WQ, :].astype(F32)
            bias = bias + window_mask(window) * LOG2E
            bias_ref[:, rows, :] = bias
        elif fresh:
            bias = (bias_ref[:, rows, :] + window_mask(window)) * LOG2E
            bias_ref[:, rows, :] = bias
        else:
            bias = bias_ref[:, rows, :]
        return mm_nt(tall, keys) + bias.reshape(HA * WQ, WK)

    def soft(logits):
        return jnp.exp2(logits - jnp.max(logits, axis=-1, keepdims=True)).astype(BF16)

    def mix(layer, window, weights):
        first = PAD + window * WQ
        values = jnp.concatenate(
            [kv_ref[layer % 2, 1, first - RIM : first - RIM + WK, :], jnp.ones((WK, channels), BF16)], axis=1
        )
        both = jnp.where(both_heads, mm(weights, values), 0.0)
        joined = both[0:WQ]
        for head in range(1, HA):
            joined = joined + both[head * WQ : (head + 1) * WQ]
        mix_ref[first : first + WQ, :] = (joined[:, :channels] / joined[:, channels:]).astype(BF16)

    def attend_steps(layer, which, fresh=False):
        def one(window):
            wt_ref[window + SPARE[0]] = soft(score(layer, window, fresh))

        return [functools.partial(one, window) for window in which] + [
            lambda window=window: mix(layer, window, wt_ref[window + SPARE[0]]) for window in which
        ]

    def attend_all(layer, which, fresh=False):
        together(attend_steps(layer, which, fresh))

    def together(*works):
        steps = [((i + 0.5) / len(work), k, step) for k, work in enumerate(works) for i, step in enumerate(work)]
        for _, _, step in sorted(steps, key=lambda entry: entry[:2]):
            step()

    def rows_of(ref, ranges):
        parts = [ref[a:b] for a, b in ranges]
        return parts[0] if len(parts) == 1 else jnp.concatenate(parts, axis=0)

    def write_rows(ref, ranges, values):
        first = 0
        for a, b in ranges:
            ref[a:b] = values[first : first + b - a]
            first += b - a

    def bits(ranges, most):
        return [piece for a, b in ranges for piece in pieces(a, b, most)]

    def norm(layer, which, ranges):
        gain = gains_ref[layer, which : which + 1]
        if sum(b - a for a, b in ranges) > atoms_dev:
            for a, b in ranges:
                h_ref[a:b] = row_norm(x_ref[a:b], gain).astype(BF16)
        else:
            for a, b in bits(ranges, NORM_ROWS):
                h_ref[a:b] = layer_norm(x_ref[a:b], gain).astype(BF16)

    def project(layer, ranges):
        side = layer % 2
        norm(layer, 0, ranges)
        out = mm(rows_of(h_ref, ranges), qkv_w[layer])
        write_rows(q_ref.at[side], ranges, (out[:, :channels] * (LOG2E * head_size ** (-0.5))).astype(BF16))
        for kind in range(2):
            write_rows(
                kv_ref.at[side, kind], ranges, out[:, (kind + 1) * channels : (kind + 2) * channels].astype(BF16)
            )

    def transition_steps(layer, ranges, keep):
        hidden = gate_ref.shape[1] // 2

        def attach():
            write_rows(x_ref, ranges, rows_of(x_ref, ranges) + mm(rows_of(mix_ref, ranges), o_w[layer]))

        def spread_out():
            write_rows(gate_ref, ranges, mm(rows_of(h_ref, ranges), up_ref[layer]))

        def gated(a, b):
            gate = 0.5 * gate_ref[a:b, :hidden]
            product = (gate + gate * jnp.tanh(gate)) * gate_ref[a:b, hidden:]
            hidden_ref[a:b] = product.astype(BF16)

        def finish():
            keep(ranges, rows_of(x_ref, ranges) + mm(rows_of(hidden_ref, ranges), down_ref[layer]))

        steps = [attach, lambda: norm(layer, 1, ranges), spread_out]
        steps += [functools.partial(gated, a, b) for a, b in bits(ranges, GATE_ROWS)]
        return steps + [finish]

    def transition(layer, ranges, keep):
        together(transition_steps(layer, ranges, keep))

    def keep_x(ranges, rows):
        write_rows(x_ref, ranges, rows)

    def advance(layer, ranges):
        transition(layer, ranges, keep_x)
        project(layer + 1, ranges)

    def outside(layer):
        side = layer % 2

        def clear_rows(first):
            for kind in range(2):
                kv_ref[side, kind, first : first + PAD] = jnp.zeros((PAD, channels), BF16)

        pl.when(jnp.logical_not(there(-1)))(lambda: clear_rows(0))
        pl.when(jnp.logical_not(there(1)))(lambda: clear_rows(PAD + atoms_dev))

    def whole(layer, step):
        spare, kept = SPARE[step], KEPT[step]
        attend_all(layer, range(-spare, windows + spare))
        advance(layer, [(PAD - kept, PAD + atoms_dev + kept)])
        outside(layer + 1)

    gains_load.wait()
    atoms_load.wait()
    for copy in qkv_loads:
        copy.wait()
    pool_loads = [load(8, to_token_hbm, to_token_ref), load(9, s_cond_hbm, s_cond_ref)]
    tp_load = load(10, token_proj_hbm, tp_ref)
    pair_load = load(11, pair_hbm, pair_ref)
    to_atom_load = load(12, to_atom_hbm, to_atom_ref)
    token_gain_load = load(18, token_gain_hbm, token_gain_ref)
    x_ref[own] = atx_ref[own].astype(F32)
    project(0, [(PAD, PAD + atoms_dev)])

    for copy in small_loads:
        copy.wait()
    mex_ref[1] = mask_ref[...].reshape(mex_ref.shape[1:])
    starts = start_ref[...].reshape(1, tokens_dev)
    rngx_ref[2, 0:1, 0:tokens_dev] = starts
    rngx_ref[2, 1:2, 0:tokens_dev] = starts + length_ref[...].reshape(1, tokens_dev)
    bias_load.wait()
    for side, first in enumerate((EDGE, EDGE + atoms_dev - bias_rows)):
        rows = bias_ref[:, first : first + bias_rows, :]
        largest = jnp.max(rows, axis=-1, keepdims=True)
        shift_ref[side] = ((rows - largest) * LOG2E).astype(BF16)
    peers = (depth - 1) + sum(jnp.where(there(offset), 1, 0) for offset in REACH)
    pl.semaphore_wait(barrier, peers)
    for sides in (mask_sides, atom_sides, bias_sides, range_sides, range_far):
        sides.start()
    inner = range(RIM // WQ + 1, windows - RIM // WQ - 1)
    attend_all(0, inner, fresh=True)
    o_load.wait()
    for copy in up_loads:
        copy.wait()
    down_load.wait()
    begin, end = PAD + inner[0] * WQ, PAD + (inner[-1] + 1) * WQ
    advance(0, [(begin, end)])
    mask_sides.receive()
    atom_sides.receive()
    beside = ((0, PAD), (PAD + atoms_dev, 2 * PAD + atoms_dev))
    for a, b in beside:
        x_ref[a:b] = atx_ref[a:b].astype(F32)
    project(0, beside)
    attend_all(0, [w for w in range(windows) if w not in inner], fresh=True)
    bias_sides.receive()
    attend_all(0, [w for w in range(-SPARE[0], windows + SPARE[0]) if w < 0 or w >= windows], fresh=True)
    advance(0, [(PAD - KEPT[0], begin), (end, PAD + atoms_dev + KEPT[0])])
    outside(1)
    whole(1, 1)

    def keep_encoded(group, rows):
        keep_x(group, rows)
        write_rows(encx_ref.at[1], [(a - PAD, b - PAD) for a, b in group], rows.astype(BF16))

    attend_all(2, range(*enc_marks[0:2]))
    for part in range(ENC_PARTS):
        a, b = enc_rows[part]
        work = transition_steps(2, [(PAD + a, PAD + b)], keep_encoded)
        if part + 1 < ENC_PARTS:
            together(attend_steps(2, range(*enc_marks[part + 1 : part + 3])), work)
        else:
            together(work)
        enc_sides[part].start()

    range_sides.receive()
    range_far.receive()
    for copy in pool_loads:
        copy.wait()
    token_gain_load.wait()
    eye = head_mask(tokens_dev, 1, tokens_dev, 1)

    def column(line):
        return jnp.sum(jnp.where(eye, line.astype(F32), 0.0), axis=1, keepdims=True)

    start_col = column(rngx_ref[2, 0:1, 0:tokens_dev])
    end_col = column(rngx_ref[2, 1:2, 0:tokens_dev])

    def pooled(blocks, low, high):
        rows = jnp.concatenate([encx_ref[block, low:high] for block in blocks], axis=0)
        projected = jnp.maximum(mm(rows, to_token_ref[...]), 0.0).astype(BF16)
        place = jnp.concatenate(
            [
                (me + block - 1) * atoms_dev
                + low
                + lax.broadcasted_iota(jnp.int32, (tokens_dev, high - low), 1)
                for block in blocks
            ],
            axis=1,
        ).astype(F32)
        member = jnp.where((place >= start_col) & (place < end_col), 1.0, 0.0).astype(BF16)
        return mm(member, projected)

    totals = pooled((1,), 0, atoms_dev)
    for part in range(ENC_PARTS):
        enc_sides[part].receive()
        totals = totals + pooled((0, 2), *enc_rows[part])
    features = totals / (end_col - start_col) + s_cond_ref[...].astype(F32)
    feat_ref[...] = features
    uall_ref[me] = layer_norm(features, token_gain_ref[...].reshape(1, width)).astype(BF16)

    def at(z, y, c):
        return (z * 2 + y) * 2 + c

    u_rows = tokens_dev // U_PARTS

    def u_copy(index, part, target, send):
        rows = uall_ref.at[index, pl.ds(part * u_rows, u_rows)]
        return pltpu.make_async_remote_copy(
            rows, rows, send, u_recv.at[index, part], device_id={"seq": target}, device_id_type=MESH
        )

    def u_arrived(index, part):
        u_copy(index, part, core_peer, c_send.at[0, 0, part]).wait_recv()

    def z_copy(z, part):
        return u_copy(me, part, at(z, row_y, core), z_send.at[z, part])

    def y_copy(z, part):
        return u_copy(at(z, row_y, core), part, y_peer, y_send.at[z, part])

    def c_copy(z, kind, part):
        return u_copy(at(z, (row_y + kind) % 2, core), part, core_peer, c_send.at[kind, z, part])

    def start(copy, *place):
        for part in range(U_PARTS):
            copy(*place, part).start()

    def sent(copy, *place):
        for part in range(U_PARTS):
            copy(*place, part).wait_send()

    shorter = jnp.minimum(row_z, depth - 1 - row_z)
    upward = jnp.where(depth - 1 - row_z > row_z, 1, -1)

    def order(step):
        turn = jnp.where(step % 2 == 1, (step + 1) // 2, -(step // 2))
        return row_z + jnp.where(step <= 2 * shorter, turn, upward * (step - shorter))

    def near_sends(step):
        start(z_copy, order(step))

    at_end = shorter == 0
    inside = jnp.logical_not(at_end)
    start(y_copy, row_z)
    if depth > 1:
        near_sends(1)
    if depth > 2:
        pl.when(inside)(lambda: near_sends(2))
    start(c_copy, row_z, 0)

    def relay(z):
        for part in range(U_PARTS):
            u_arrived(at(z, row_y, core), part)
            y_copy(z, part).start()
            c_copy(z, 0, part).start()

    def across(z):
        for part in range(U_PARTS):
            u_arrived(at(z, 1 - row_y, core), part)
            c_copy(z, 1, part).start()

    tp_load.wait()
    team = HT // TEAMS
    team_rows, team_width = team * tokens_dev, width // TEAMS
    token_heads = head_mask(team_rows, tokens_dev, team_width, token_head)
    query = mm(uall_ref[me], tp_ref[0]).astype(BF16)
    for part in range(TEAMS):
        cols = slice(part * team_width, (part + 1) * team_width)
        apart = jnp.where(
            token_heads, jnp.concatenate([query[:, cols]] * team, axis=0), jnp.zeros((), BF16)
        )
        folded = mm_nt(apart, tp_ref[1, :, cols]) * token_head ** (-0.5)
        qk_ref[part * team_rows : (part + 1) * team_rows] = folded.astype(BF16)
    max_ref[...] = jnp.full_like(max_ref, -1e30)
    acc_ref[...] = jnp.zeros_like(acc_ref)
    pair_load.wait()
    span = 4 * tokens_dev

    def token_block(places):
        rows = jnp.concatenate(
            [uall_ref[pl.ds(at(z, y, 0), 2)].reshape(2 * tokens_dev, width) for z, y in places], axis=0
        )
        bias = jnp.concatenate(
            [
                pair_ref[:, :, pl.ds(pl.multiple_of(at(z, y, 0) * tokens_dev, 2 * tokens_dev), 2 * tokens_dev)]
                for z, y in places
            ],
            axis=2,
        )
        bias = bias.reshape(HT * tokens_dev, span).astype(F32)
        logits = mm_nt(qk_ref[...], rows) + bias
        before = max_ref[...]
        now = jnp.maximum(before, jnp.max(logits, axis=-1, keepdims=True))
        max_ref[...] = now
        weights = jnp.exp(logits - jnp.concatenate([now] * (span // LANES), axis=1)).astype(BF16)
        shrink = jnp.exp(before - now)
        values = mm(rows, tp_ref[2]).astype(BF16)
        for part in range(TEAMS):
            lines = slice(part * team_rows, (part + 1) * team_rows)
            ones = jnp.ones((span, acc_ref.shape[1] - team_width), BF16)
            beside = jnp.concatenate([values[:, part * team_width : (part + 1) * team_width], ones], axis=1)
            scale = jnp.concatenate([shrink[lines]] * (acc_ref.shape[1] // LANES), axis=1)
            acc_ref[lines] = acc_ref[lines] * scale + mm(weights[lines], beside)

    if depth > 1:
        sent(z_copy, order(1))
    if depth > 2:
        pl.when(at_end)(lambda: near_sends(2))
    if depth > 3:
        pl.when(inside)(lambda: near_sends(3))
    across(order(0))
    if depth > 1:
        relay(order(1))

    def far_sends():
        sent(z_copy, order(2))
        near_sends(3)

    if depth > 3:
        pl.when(at_end)(far_sends)
    for step in range(4, depth):
        near_sends(step)

    def other_core(step, kind):
        for part in range(U_PARTS):
            u_arrived(at(order(step), (row_y + kind) % 2, 1 - core), part)

    def token_pairs(step, kind):
        token_block([(order(step + i), (row_y + kind) % 2) for i in range(2)])

    def token_step(turn, carry):
        step = 2 * turn
        other_core(step, 0)
        other_core(step + 1, 0)
        token_pairs(step, 0)
        pl.when(step + 2 < depth)(lambda: relay(order(step + 2)))
        across(order(step + 1))
        pl.when(step + 3 < depth)(lambda: relay(order(step + 3)))
        other_core(step, 1)
        other_core(step + 1, 1)
        token_pairs(step, 1)
        pl.when(step + 2 < depth)(lambda: across(order(step + 2)))
        return carry

    lax.fori_loop(0, depth // 2, token_step, 0)

    parts = []
    for part in range(TEAMS):
        lines = slice(part * team_rows, (part + 1) * team_rows)
        mixed = acc_ref[lines, 0:team_width] * (1.0 / acc_ref[lines, team_width : team_width + 1])
        mixed = jnp.where(token_heads, mixed, 0.0)
        joined = mixed[0:tokens_dev]
        for head in range(1, team):
            joined = joined + mixed[head * tokens_dev : (head + 1) * tokens_dev]
        parts.append(joined.astype(BF16))
    token_mix = jnp.concatenate(parts, axis=1)
    updated = feat_ref[...] + mm(token_mix, tp_ref[3])
    to_atom_load.wait()
    rowsx_ref[2] = mm(updated.astype(BF16), to_atom_ref[...]).astype(BF16)
    row_sides.start()
    row_far.start()

    areas = ((0, PAD, 0), (PAD, PAD + atoms_dev, 1), (PAD + atoms_dev, 2 * PAD + atoms_dev, 2))

    def members(low, high, slot):
        shape = (high - low, 3 * tokens_dev)
        place = me * atoms_dev + low - PAD + lax.broadcasted_iota(jnp.int32, shape, 0)
        place = place.astype(F32)
        first, end = (
            jnp.concatenate([rngx_ref[slot + i, k : k + 1, 0:tokens_dev] for i in range(3)], axis=1).astype(F32)
            for k in range(2)
        )
        return jnp.where((place >= first) & (place < end), 1.0, 0.0).astype(BF16)

    x_ref[0:PAD] = encx_ref[0, atoms_dev - PAD : atoms_dev].astype(F32)
    x_ref[PAD + atoms_dev :] = encx_ref[2, 0:PAD].astype(F32)
    belongs = [members(*area) for area in areas]
    for sides in (mask_sides, range_sides, range_far, atom_sides, bias_sides, *enc_sides):
        sides.sent()
    if depth == 3:
        sent(z_copy, order(2))
    elif depth > 3:
        pl.when(inside)(lambda: sent(z_copy, order(2)))
    for step in range(depth):
        if step > 2:
            sent(z_copy, order(step))
        sent(y_copy, step)
        sent(c_copy, step, 0)
        sent(c_copy, step, 1)
    row_sides.receive()
    row_far.receive()
    for belong, (low, high, slot) in zip(belongs, areas):
        tall_rows = rowsx_ref[slot : slot + 3].reshape(3 * tokens_dev, channels)
        x_ref[low:high] = x_ref[low:high] + mm(belong, tall_rows)

    project(HALF, [(0, atoms_dev + 2 * PAD)])
    outside(HALF)
    whole(HALF, 0)
    whole(HALF + 1, 1)

    def keep_decoded(group, rows):
        for a, b in group:
            out_ref[0, a - PAD : b - PAD] = rows.astype(BF16)

    attend_all(HALF + 2, range(windows))
    transition(HALF + 2, [(PAD, PAD + atoms_dev)], keep_decoded)

    row_sides.sent()
    row_far.sent()


def shards(
    count,
    atoms,
    s_cond,
    token_start,
    token_len,
    atom_mask,
    atom_bias,
    pair_bias,
    atom_proj,
    atom_up,
    atom_down,
    atom_gains,
    to_token,
    token_proj,
    token_gain,
    to_atom,
):
    atoms_dev, channels = atoms.shape[1:]
    tokens_dev, width = s_cond.shape
    layers = 2 * HALF
    vmem = pl.BlockSpec(memory_space=pltpu.VMEM)
    hbm = pl.BlockSpec(memory_space=pl.ANY)
    depth = count // 4
    spread = atoms_dev + 2 * PAD
    return pl.pallas_call(
        functools.partial(kernel, count),
        out_shape=pltpu.VMEM(atoms.shape, BF16),
        in_specs=[hbm] * 15,
        out_specs=vmem,
        scratch_shapes=[
            pltpu.VMEM(token_start.shape, jnp.int32),
            pltpu.VMEM(token_len.shape, jnp.int32),
            pltpu.VMEM(atom_mask.shape, jnp.int32),
            pltpu.VMEM(atom_gains.shape, F32),
            pltpu.VMEM(token_gain.shape, F32),
            pltpu.VMEM((spread, channels), BF16),
            pltpu.VMEM((spread, channels), F32),
            pltpu.VMEM((2, 2, spread, channels), BF16),
            pltpu.VMEM((2, spread, channels), BF16),
            pltpu.VMEM((spread, channels), BF16),
            pltpu.VMEM((spread, channels), BF16),
            pltpu.VMEM((spread, 2 * atom_up.shape[3]), F32),
            pltpu.VMEM((spread, atom_up.shape[3]), BF16),
            pltpu.VMEM((HA, atoms_dev + 2 * EDGE, WK), F32),
            pltpu.VMEM((2, HA, EDGE - WQ + RIM % WQ, WK), BF16),
            pltpu.VMEM((2, HA, EDGE, WK), BF16),
            pltpu.VMEM(pair_bias.shape, BF16),
            pltpu.VMEM((layers, channels, 3 * channels), BF16),
            pltpu.VMEM((layers, channels, channels), BF16),
            pltpu.VMEM((layers, channels, 2 * atom_up.shape[3]), BF16),
            pltpu.VMEM(atom_down.shape, BF16),
            pltpu.VMEM(to_token.shape, BF16),
            pltpu.VMEM(to_atom.shape, BF16),
            pltpu.VMEM(s_cond.shape, BF16),
            pltpu.VMEM(token_proj.shape, BF16),
            pltpu.VMEM((3, atoms_dev // LANES, LANES), jnp.int32),
            pltpu.VMEM((atoms_dev // WQ + 2 * SPARE[0], HA * WQ, WK), BF16),
            pltpu.VMEM((5, 8, pl.cdiv(tokens_dev, LANES) * LANES), jnp.int32),
            pltpu.VMEM((3, atoms_dev, channels), BF16),
            pltpu.VMEM((5, tokens_dev, channels), BF16),
            pltpu.VMEM((count, tokens_dev, width), BF16),
            pltpu.VMEM((tokens_dev, width), F32),
            pltpu.VMEM((HT * tokens_dev, width), BF16),
            pltpu.VMEM((HT * tokens_dev, pl.cdiv(width // TEAMS + 1, LANES) * LANES), F32),
            pltpu.VMEM((HT * tokens_dev, LANES), F32),
            pltpu.SemaphoreType.DMA((19,)),
            pltpu.SemaphoreType.DMA((7, 2)),
            pltpu.SemaphoreType.DMA((7, 2)),
            pltpu.SemaphoreType.DMA((2, 2)),
            pltpu.SemaphoreType.DMA((2, 2)),
            pltpu.SemaphoreType.DMA((depth, U_PARTS)),
            pltpu.SemaphoreType.DMA((depth, U_PARTS)),
            pltpu.SemaphoreType.DMA((2, depth, U_PARTS)),
            pltpu.SemaphoreType.DMA((count, U_PARTS)),
        ],
        compiler_params=pltpu.CompilerParams(
            collective_id=0, has_side_effects=True, vmem_limit_bytes=60 * 1024 * 1024
        ),
    )(
        atoms,
        s_cond,
        token_start,
        token_len,
        atom_mask,
        atom_bias,
        pair_bias,
        atom_proj,
        atom_up,
        atom_down,
        atom_gains,
        to_token,
        token_proj,
        token_gain,
        to_atom,
    )


def solution(mesh):
    placed = (
        P("groups", "seq", None),
        P(("groups", "seq"), None),
        P(("groups", "seq")),
        P(("groups", "seq")),
        P(("groups", "seq")),
        P("groups", "seq", None),
        P("groups", "seq", None),
        P(),
        P(),
        P(),
        P(),
        P(),
        P(),
        P(),
        P(),
    )
    return jax.shard_map(
        functools.partial(shards, mesh.shape["seq"]),
        mesh=mesh,
        in_specs=placed,
        out_specs=P("groups", "seq", None),
        check_vma=False,
    )
```

```python
import functools

import jax
import jax.numpy as jnp
from jax import lax
from jax.experimental import pallas as pl
from jax.experimental.pallas import tpu as pltpu
from jax.sharding import PartitionSpec as P

HT = 16
HA = 4
WQ = 32
WK = 128
HALF = 3
TEAMS = 4
U_PARTS = 2
RIM = (WK - WQ) // 2
LANES = 128
SPARE = (4, 2, 0)
EDGE = SPARE[0] * WQ
PAD = EDGE + RIM
KEPT = (SPARE[1] * WQ + RIM, RIM, 0)

epsilon = 1e-05
masked = -1000000000.0
LOG2E = 1.4426950408889634
MESH = pl.DeviceIdType.MESH
F32 = jnp.float32
BF16 = jnp.bfloat16

MASK, RANGE, ATOMS, BIAS, ENC, ROWS = 0, 1, 2, 3, 4, 6
ENC_SHARE = (5, 3)
ENC_PARTS = len(ENC_SHARE)
NORM_ROWS, GATE_ROWS = 64, 32
REACH = (-1, 1, -2, 2)


def layer_norm(values, gain_vec):
    average = jnp.mean(values, axis=-1, keepdims=True)
    centred = values - average
    spread = jnp.mean(centred * centred, axis=-1, keepdims=True)
    return centred * lax.rsqrt(spread + epsilon) * gain_vec


def row_mean(values):
    high = values.astype(BF16)
    low = (values - high.astype(F32)).astype(BF16)
    size = values.shape[-1]
    return mm(jnp.concatenate([high, low], axis=-1), jnp.ones((2 * size, size), BF16)) * (1.0 / size)


def row_norm(values, gain_vec):
    centred = values - row_mean(values)
    return centred * lax.rsqrt(row_mean(centred * centred) + epsilon) * gain_vec


def mm(left, right):
    return jnp.dot(left, right, preferred_element_type=F32)


def mm_nt(left, right):
    return lax.dot_general(left, right, (((1,), (1,)), ((), ())), preferred_element_type=F32)


def head_mask(rows, row_size, cols, col_size):
    row_head = lax.broadcasted_iota(jnp.int32, (rows, cols), 0) // row_size
    col_head = lax.broadcasted_iota(jnp.int32, (rows, cols), 1) // col_size
    return row_head == col_head


def pieces(low, high, most):
    units = (high - low) // 16
    number = pl.cdiv(high - low, most)
    marks = [low + 16 * (units * i // number) for i in range(number)] + [high]
    return list(zip(marks[:-1], marks[1:]))


def kernel(
    count,
    atoms_hbm,
    s_cond_hbm,
    start_hbm,
    length_hbm,
    mask_hbm,
    bias_hbm,
    pair_hbm,
    proj_hbm,
    up_hbm,
    down_hbm,
    gains_hbm,
    to_token_hbm,
    token_proj_hbm,
    token_gain_hbm,
    to_atom_hbm,
    out_ref,
    start_ref,
    length_ref,
    mask_ref,
    gains_ref,
    token_gain_ref,
    atx_ref,
    x_ref,
    kv_ref,
    q_ref,
    mix_ref,
    h_ref,
    gate_ref,
    hidden_ref,
    bias_ref,
    shift_ref,
    beyond_ref,
    pair_ref,
    qkv_w,
    o_w,
    up_ref,
    down_ref,
    to_token_ref,
    to_atom_ref,
    s_cond_ref,
    tp_ref,
    mex_ref,
    wt_ref,
    rngx_ref,
    encx_ref,
    rowsx_ref,
    uall_ref,
    feat_ref,
    qk_ref,
    acc_ref,
    max_ref,
    load_sem,
    side_send,
    side_recv,
    far_send,
    far_recv,
    z_send,
    y_send,
    c_send,
    u_recv,
):
    me = lax.axis_index("seq")
    core = lax.rem(me, 2)
    row_y = lax.rem(me // 2, 2)
    row_z = me // 4
    depth = count // 4
    atoms_dev = atoms_hbm.shape[1]
    channels = atoms_hbm.shape[2]
    tokens_dev, width = s_cond_ref.shape
    windows = atoms_dev // WQ
    head_size = channels // HA
    token_head = width // HT
    core_peer = me + 1 - 2 * core
    y_peer = me + 2 - 4 * row_y
    own = slice(PAD, PAD + atoms_dev)
    bias_rows = EDGE - WQ + RIM % WQ

    def there(offset):
        return me + offset >= 0 if offset < 0 else me + offset < count

    def load(index, source, target):
        copy = pltpu.make_async_copy(source, target, load_sem.at[index])
        copy.start()
        return copy

    gains_load = load(14, gains_hbm, gains_ref)
    atoms_load = load(0, atoms_hbm.at[0], atx_ref.at[pl.ds(PAD, atoms_dev)])
    qkv_loads = [
        load(1 + k, proj_hbm.at[:, k], qkv_w.at[:, :, pl.ds(k * channels, channels)]) for k in range(3)
    ]
    bias_load = load(4, bias_hbm, bias_ref.at[:, pl.ds(EDGE, atoms_dev)])
    small_loads = [
        load(15, mask_hbm, mask_ref),
        load(16, start_hbm, start_ref),
        load(17, length_hbm, length_ref),
    ]

    barrier = pltpu.get_barrier_semaphore()

    def greet(target):
        pl.semaphore_signal(barrier, inc=1, device_id={"seq": target}, device_id_type=MESH)

    for offset in REACH:
        pl.when(there(offset))(lambda: greet(me + offset))
    for z in range(depth):
        pl.when(row_z != z)(lambda: greet(me + 4 * (z - row_z)))

    o_load = load(5, proj_hbm.at[:, 3], o_w)
    hidden_units = up_hbm.shape[3]
    up_loads = [
        load(6 + 7 * k, up_hbm.at[:, k], up_ref.at[:, :, pl.ds(k * hidden_units, hidden_units)]) for k in range(2)
    ]
    down_load = load(7, down_hbm, down_ref)
    def zero(ref, slot):
        ref[slot] = jnp.zeros(ref.shape[1:], ref.dtype)

    def clear_near(side):
        for ref in (mex_ref, encx_ref):
            zero(ref, 2 * side)
        for ref in (rngx_ref, rowsx_ref):
            zero(ref, 1 + 2 * side)
        rows = slice(0, PAD) if side == 0 else slice(PAD + atoms_dev, 2 * PAD + atoms_dev)
        atx_ref[rows] = jnp.zeros((PAD, channels), BF16)
        zero(beyond_ref, side)

    def clear_far(side):
        for ref in (rngx_ref, rowsx_ref):
            zero(ref, 4 * side)

    for side in range(2):
        sign = 2 * side - 1
        pl.when(jnp.logical_not(there(sign)))(lambda: clear_near(side))
        pl.when(jnp.logical_not(there(2 * sign)))(lambda: clear_far(side))
    beyond_ref[0, :, 0 : EDGE - bias_rows] = jnp.zeros((HA, EDGE - bias_rows, WK), BF16)
    beyond_ref[1, :, bias_rows:] = jnp.zeros((HA, EDGE - bias_rows, WK), BF16)

    class Sides:
        def __init__(self, reach, send, recv, to_left, to_right):
            self.reach = reach
            self.copies = [
                pltpu.make_async_remote_copy(
                    source, target, send(i), recv(i), device_id={"seq": me + sign * reach}, device_id_type=MESH
                )
                for i, (sign, (source, target)) in enumerate(zip((-1, 1), (to_left, to_right)))
            ]

        def start(self):
            pl.when(there(-self.reach))(lambda: self.copies[0].start())
            pl.when(there(self.reach))(lambda: self.copies[1].start())

        def receive(self):
            pl.when(there(self.reach))(lambda: self.copies[0].wait_recv())
            pl.when(there(-self.reach))(lambda: self.copies[1].wait_recv())

        def sent(self):
            pl.when(there(-self.reach))(lambda: self.copies[0].wait_send())
            pl.when(there(self.reach))(lambda: self.copies[1].wait_send())

    def near(kind, to_left, to_right):
        return Sides(1, lambda i: side_send.at[kind, i], lambda i: side_recv.at[kind, i], to_left, to_right)

    def far(kind, to_left, to_right):
        return Sides(2, lambda i: far_send.at[kind, i], lambda i: far_recv.at[kind, i], to_left, to_right)

    mask_sides = near(MASK, (mex_ref.at[1], mex_ref.at[2]), (mex_ref.at[1], mex_ref.at[0]))
    range_sides = near(RANGE, (rngx_ref.at[2], rngx_ref.at[3]), (rngx_ref.at[2], rngx_ref.at[1]))
    range_far = far(0, (rngx_ref.at[2], rngx_ref.at[4]), (rngx_ref.at[2], rngx_ref.at[0]))
    row_sides = near(ROWS, (rowsx_ref.at[2], rowsx_ref.at[3]), (rowsx_ref.at[2], rowsx_ref.at[1]))
    row_far = far(1, (rowsx_ref.at[2], rowsx_ref.at[4]), (rowsx_ref.at[2], rowsx_ref.at[0]))
    atom_sides = near(
        ATOMS,
        (atoms_hbm.at[0, pl.ds(0, PAD)], atx_ref.at[pl.ds(PAD + atoms_dev, PAD)]),
        (atoms_hbm.at[0, pl.ds(atoms_dev - PAD, PAD)], atx_ref.at[pl.ds(0, PAD)]),
    )
    bias_sides = near(
        BIAS,
        (shift_ref.at[0], beyond_ref.at[1, :, pl.ds(0, bias_rows)]),
        (shift_ref.at[1], beyond_ref.at[0, :, pl.ds(EDGE - bias_rows, bias_rows)]),
    )
    enc_marks = [windows * sum(ENC_SHARE[:part]) // sum(ENC_SHARE) for part in range(ENC_PARTS + 1)]
    enc_rows = [(WQ * a, WQ * b) for a, b in zip(enc_marks[:-1], enc_marks[1:])]

    def enc_part(part):
        rows = pl.ds(enc_rows[part][0], enc_rows[part][1] - enc_rows[part][0])
        return near(
            ENC + part,
            (encx_ref.at[1, rows], encx_ref.at[2, rows]),
            (encx_ref.at[1, rows], encx_ref.at[0, rows]),
        )

    enc_sides = [enc_part(part) for part in range(ENC_PARTS)]

    mask_lines = atoms_dev // LANES

    def mask_row(index):
        return mex_ref[index // mask_lines, index % mask_lines : index % mask_lines + 1, :]

    def window_mask(window):
        first = atoms_dev + window * WQ - RIM
        row, offset = first // LANES, first % LANES
        line = mask_row(row)
        if offset:
            line = jnp.concatenate([line[:, offset:], mask_row(row + 1)[:, :offset]], axis=1)
        return jnp.where(line == 1, 0.0, masked).astype(F32)

    atom_heads = head_mask(HA * WQ, WQ, channels, head_size)


    both_heads = jnp.concatenate([atom_heads] * 2, axis=1)

    def score(layer, window, fresh):
        first = PAD + window * WQ
        query = q_ref[layer % 2, first : first + WQ, :]
        tall = jnp.where(atom_heads, jnp.concatenate([query] * HA, axis=0), jnp.zeros((), BF16))
        keys = kv_ref[layer % 2, 0, first - RIM : first - RIM + WK, :]
        rows = slice(EDGE + window * WQ, EDGE + window * WQ + WQ)
        if fresh and not 0 <= window < windows:
            side, near_row = (0, EDGE + window * WQ) if window < 0 else (1, window * WQ - atoms_dev)
            bias = beyond_ref[side, :, near_row : near_row + WQ, :].astype(F32)
            bias = bias + window_mask(window) * LOG2E
            bias_ref[:, rows, :] = bias
        elif fresh:
            bias = (bias_ref[:, rows, :] + window_mask(window)) * LOG2E
            bias_ref[:, rows, :] = bias
        else:
            bias = bias_ref[:, rows, :]
        return mm_nt(tall, keys) + bias.reshape(HA * WQ, WK)

    def soft(logits):
        return jnp.exp2(logits - jnp.max(logits, axis=-1, keepdims=True)).astype(BF16)

    def mix(layer, window, weights):
        first = PAD + window * WQ
        values = jnp.concatenate(
            [kv_ref[layer % 2, 1, first - RIM : first - RIM + WK, :], jnp.ones((WK, channels), BF16)], axis=1
        )
        both = jnp.where(both_heads, mm(weights, values), 0.0)
        joined = both[0:WQ]
        for head in range(1, HA):
            joined = joined + both[head * WQ : (head + 1) * WQ]
        mix_ref[first : first + WQ, :] = (joined[:, :channels] / joined[:, channels:]).astype(BF16)

    def attend_steps(layer, which, fresh=False):
        def one(window):
            wt_ref[window + SPARE[0]] = soft(score(layer, window, fresh))

        return [functools.partial(one, window) for window in which] + [
            lambda window=window: mix(layer, window, wt_ref[window + SPARE[0]]) for window in which
        ]

    def attend_all(layer, which, fresh=False):
        together(attend_steps(layer, which, fresh))

    def together(*works):
        steps = [((i + 0.5) / len(work), k, step) for k, work in enumerate(works) for i, step in enumerate(work)]
        for _, _, step in sorted(steps, key=lambda entry: entry[:2]):
            step()

    def rows_of(ref, ranges):
        parts = [ref[a:b] for a, b in ranges]
        return parts[0] if len(parts) == 1 else jnp.concatenate(parts, axis=0)

    def write_rows(ref, ranges, values):
        first = 0
        for a, b in ranges:
            ref[a:b] = values[first : first + b - a]
            first += b - a

    def bits(ranges, most):
        return [piece for a, b in ranges for piece in pieces(a, b, most)]

    def norm(layer, which, ranges):
        gain = gains_ref[layer, which : which + 1]
        if sum(b - a for a, b in ranges) > atoms_dev:
            for a, b in ranges:
                h_ref[a:b] = row_norm(x_ref[a:b], gain).astype(BF16)
        else:
            for a, b in bits(ranges, NORM_ROWS):
                h_ref[a:b] = layer_norm(x_ref[a:b], gain).astype(BF16)

    def project(layer, ranges):
        side = layer % 2
        norm(layer, 0, ranges)
        out = mm(rows_of(h_ref, ranges), qkv_w[layer])
        write_rows(q_ref.at[side], ranges, (out[:, :channels] * (LOG2E * head_size ** (-0.5))).astype(BF16))
        for kind in range(2):
            write_rows(
                kv_ref.at[side, kind], ranges, out[:, (kind + 1) * channels : (kind + 2) * channels].astype(BF16)
            )

    def transition_steps(layer, ranges, keep):
        hidden = gate_ref.shape[1] // 2

        def attach():
            write_rows(x_ref, ranges, rows_of(x_ref, ranges) + mm(rows_of(mix_ref, ranges), o_w[layer]))

        def spread_out():
            write_rows(gate_ref, ranges, mm(rows_of(h_ref, ranges), up_ref[layer]))

        def gated(a, b):
            gate = 0.5 * gate_ref[a:b, :hidden]
            product = (gate + gate * jnp.tanh(gate)) * gate_ref[a:b, hidden:]
            hidden_ref[a:b] = product.astype(BF16)

        def finish():
            keep(ranges, rows_of(x_ref, ranges) + mm(rows_of(hidden_ref, ranges), down_ref[layer]))

        steps = [attach, lambda: norm(layer, 1, ranges), spread_out]
        steps += [functools.partial(gated, a, b) for a, b in bits(ranges, GATE_ROWS)]
        return steps + [finish]

    def transition(layer, ranges, keep):
        together(transition_steps(layer, ranges, keep))

    def keep_x(ranges, rows):
        write_rows(x_ref, ranges, rows)

    def advance(layer, ranges):
        transition(layer, ranges, keep_x)
        project(layer + 1, ranges)

    def outside(layer):
        side = layer % 2

        def clear_rows(first):
            for kind in range(2):
                kv_ref[side, kind, first : first + PAD] = jnp.zeros((PAD, channels), BF16)

        pl.when(jnp.logical_not(there(-1)))(lambda: clear_rows(0))
        pl.when(jnp.logical_not(there(1)))(lambda: clear_rows(PAD + atoms_dev))

    def whole(layer, step):
        spare, kept = SPARE[step], KEPT[step]
        attend_all(layer, range(-spare, windows + spare))
        advance(layer, [(PAD - kept, PAD + atoms_dev + kept)])
        outside(layer + 1)

    gains_load.wait()
    atoms_load.wait()
    for copy in qkv_loads:
        copy.wait()
    pool_loads = [load(8, to_token_hbm, to_token_ref), load(9, s_cond_hbm, s_cond_ref)]
    tp_load = load(10, token_proj_hbm, tp_ref)
    pair_load = load(11, pair_hbm, pair_ref)
    to_atom_load = load(12, to_atom_hbm, to_atom_ref)
    token_gain_load = load(18, token_gain_hbm, token_gain_ref)
    x_ref[own] = atx_ref[own].astype(F32)
    project(0, [(PAD, PAD + atoms_dev)])

    for copy in small_loads:
        copy.wait()
    mex_ref[1] = mask_ref[...].reshape(mex_ref.shape[1:])
    starts = start_ref[...].reshape(1, tokens_dev)
    rngx_ref[2, 0:1, 0:tokens_dev] = starts
    rngx_ref[2, 1:2, 0:tokens_dev] = starts + length_ref[...].reshape(1, tokens_dev)
    bias_load.wait()
    for side, first in enumerate((EDGE, EDGE + atoms_dev - bias_rows)):
        rows = bias_ref[:, first : first + bias_rows, :]
        largest = jnp.max(rows, axis=-1, keepdims=True)
        shift_ref[side] = ((rows - largest) * LOG2E).astype(BF16)
    peers = (depth - 1) + sum(jnp.where(there(offset), 1, 0) for offset in REACH)
    pl.semaphore_wait(barrier, peers)
    for sides in (mask_sides, atom_sides, bias_sides, range_sides, range_far):
        sides.start()
    inner = range(RIM // WQ + 1, windows - RIM // WQ - 1)
    attend_all(0, inner, fresh=True)
    o_load.wait()
    for copy in up_loads:
        copy.wait()
    down_load.wait()
    begin, end = PAD + inner[0] * WQ, PAD + (inner[-1] + 1) * WQ
    advance(0, [(begin, end)])
    mask_sides.receive()
    atom_sides.receive()
    beside = ((0, PAD), (PAD + atoms_dev, 2 * PAD + atoms_dev))
    for a, b in beside:
        x_ref[a:b] = atx_ref[a:b].astype(F32)
    project(0, beside)
    attend_all(0, [w for w in range(windows) if w not in inner], fresh=True)
    bias_sides.receive()
    attend_all(0, [w for w in range(-SPARE[0], windows + SPARE[0]) if w < 0 or w >= windows], fresh=True)
    advance(0, [(PAD - KEPT[0], begin), (end, PAD + atoms_dev + KEPT[0])])
    outside(1)
    whole(1, 1)

    def keep_encoded(group, rows):
        keep_x(group, rows)
        write_rows(encx_ref.at[1], [(a - PAD, b - PAD) for a, b in group], rows.astype(BF16))

    attend_all(2, range(*enc_marks[0:2]))
    for part in range(ENC_PARTS):
        a, b = enc_rows[part]
        work = transition_steps(2, [(PAD + a, PAD + b)], keep_encoded)
        if part + 1 < ENC_PARTS:
            together(attend_steps(2, range(*enc_marks[part + 1 : part + 3])), work)
        else:
            together(work)
        enc_sides[part].start()

    range_sides.receive()
    range_far.receive()
    for copy in pool_loads:
        copy.wait()
    token_gain_load.wait()
    eye = head_mask(tokens_dev, 1, tokens_dev, 1)

    def column(line):
        return jnp.sum(jnp.where(eye, line.astype(F32), 0.0), axis=1, keepdims=True)

    start_col = column(rngx_ref[2, 0:1, 0:tokens_dev])
    end_col = column(rngx_ref[2, 1:2, 0:tokens_dev])

    def pooled(blocks, low, high):
        rows = jnp.concatenate([encx_ref[block, low:high] for block in blocks], axis=0)
        projected = jnp.maximum(mm(rows, to_token_ref[...]), 0.0).astype(BF16)
        place = jnp.concatenate(
            [
                (me + block - 1) * atoms_dev
                + low
                + lax.broadcasted_iota(jnp.int32, (tokens_dev, high - low), 1)
                for block in blocks
            ],
            axis=1,
        ).astype(F32)
        member = jnp.where((place >= start_col) & (place < end_col), 1.0, 0.0).astype(BF16)
        return mm(member, projected)

    totals = pooled((1,), 0, atoms_dev)
    for part in range(ENC_PARTS):
        enc_sides[part].receive()
        totals = totals + pooled((0, 2), *enc_rows[part])
    features = totals / (end_col - start_col) + s_cond_ref[...].astype(F32)
    feat_ref[...] = features
    uall_ref[me] = layer_norm(features, token_gain_ref[...].reshape(1, width)).astype(BF16)

    def at(z, y, c):
        return (z * 2 + y) * 2 + c

    u_rows = tokens_dev // U_PARTS

    def u_copy(index, part, target, send):
        rows = uall_ref.at[index, pl.ds(part * u_rows, u_rows)]
        return pltpu.make_async_remote_copy(
            rows, rows, send, u_recv.at[index, part], device_id={"seq": target}, device_id_type=MESH
        )

    def u_arrived(index, part):
        u_copy(index, part, core_peer, c_send.at[0, 0, part]).wait_recv()

    def z_copy(z, part):
        return u_copy(me, part, at(z, row_y, core), z_send.at[z, part])

    def y_copy(z, part):
        return u_copy(at(z, row_y, core), part, y_peer, y_send.at[z, part])

    def c_copy(z, kind, part):
        return u_copy(at(z, (row_y + kind) % 2, core), part, core_peer, c_send.at[kind, z, part])

    def start(copy, *place):
        for part in range(U_PARTS):
            copy(*place, part).start()

    def sent(copy, *place):
        for part in range(U_PARTS):
            copy(*place, part).wait_send()

    shorter = jnp.minimum(row_z, depth - 1 - row_z)
    upward = jnp.where(depth - 1 - row_z > row_z, 1, -1)

    def order(step):
        turn = jnp.where(step % 2 == 1, (step + 1) // 2, -(step // 2))
        return row_z + jnp.where(step <= 2 * shorter, turn, upward * (step - shorter))

    def near_sends(step):
        start(z_copy, order(step))

    at_end = shorter == 0
    inside = jnp.logical_not(at_end)
    start(y_copy, row_z)
    if depth > 1:
        near_sends(1)
    if depth > 2:
        pl.when(inside)(lambda: near_sends(2))
    start(c_copy, row_z, 0)

    def relay(z):
        for part in range(U_PARTS):
            u_arrived(at(z, row_y, core), part)
            y_copy(z, part).start()
            c_copy(z, 0, part).start()

    def across(z):
        for part in range(U_PARTS):
            u_arrived(at(z, 1 - row_y, core), part)
            c_copy(z, 1, part).start()

    tp_load.wait()
    team = HT // TEAMS
    team_rows, team_width = team * tokens_dev, width // TEAMS
    token_heads = head_mask(team_rows, tokens_dev, team_width, token_head)
    query = mm(uall_ref[me], tp_ref[0]).astype(BF16)
    for part in range(TEAMS):
        cols = slice(part * team_width, (part + 1) * team_width)
        apart = jnp.where(
            token_heads, jnp.concatenate([query[:, cols]] * team, axis=0), jnp.zeros((), BF16)
        )
        folded = mm_nt(apart, tp_ref[1, :, cols]) * token_head ** (-0.5)
        qk_ref[part * team_rows : (part + 1) * team_rows] = folded.astype(BF16)
    max_ref[...] = jnp.full_like(max_ref, -1e30)
    acc_ref[...] = jnp.zeros_like(acc_ref)
    pair_load.wait()
    span = 4 * tokens_dev

    def token_block(places):
        rows = jnp.concatenate(
            [uall_ref[pl.ds(at(z, y, 0), 2)].reshape(2 * tokens_dev, width) for z, y in places], axis=0
        )
        bias = jnp.concatenate(
            [
                pair_ref[:, :, pl.ds(pl.multiple_of(at(z, y, 0) * tokens_dev, 2 * tokens_dev), 2 * tokens_dev)]
                for z, y in places
            ],
            axis=2,
        )
        bias = bias.reshape(HT * tokens_dev, span).astype(F32)
        logits = mm_nt(qk_ref[...], rows) + bias
        before = max_ref[...]
        now = jnp.maximum(before, jnp.max(logits, axis=-1, keepdims=True))
        max_ref[...] = now
        weights = jnp.exp(logits - jnp.concatenate([now] * (span // LANES), axis=1)).astype(BF16)
        shrink = jnp.exp(before - now)
        values = mm(rows, tp_ref[2]).astype(BF16)
        for part in range(TEAMS):
            lines = slice(part * team_rows, (part + 1) * team_rows)
            ones = jnp.ones((span, acc_ref.shape[1] - team_width), BF16)
            beside = jnp.concatenate([values[:, part * team_width : (part + 1) * team_width], ones], axis=1)
            scale = jnp.concatenate([shrink[lines]] * (acc_ref.shape[1] // LANES), axis=1)
            acc_ref[lines] = acc_ref[lines] * scale + mm(weights[lines], beside)

    if depth > 1:
        sent(z_copy, order(1))
    if depth > 2:
        pl.when(at_end)(lambda: near_sends(2))
    if depth > 3:
        pl.when(inside)(lambda: near_sends(3))
    across(order(0))
    if depth > 1:
        relay(order(1))
    if depth > 2:
        pl.when(inside)(lambda: relay(order(2)))

    def far_sends():
        sent(z_copy, order(2))
        near_sends(3)

    if depth > 3:
        pl.when(at_end)(far_sends)
    for step in range(4, depth):
        near_sends(step)

    def other_core(step, kind):
        for part in range(U_PARTS):
            u_arrived(at(order(step), (row_y + kind) % 2, 1 - core), part)

    def token_pairs(step, kind):
        token_block([(order(step + i), (row_y + kind) % 2) for i in range(2)])

    def token_step(turn, carry):
        step = 2 * turn
        other_core(step, 0)
        other_core(step + 1, 0)
        token_pairs(step, 0)
        pl.when((step + 2 < depth) & (at_end | (step > 0)))(lambda: relay(order(step + 2)))
        across(order(step + 1))
        pl.when(step + 3 < depth)(lambda: relay(order(step + 3)))
        other_core(step, 1)
        other_core(step + 1, 1)
        token_pairs(step, 1)
        pl.when(step + 2 < depth)(lambda: across(order(step + 2)))
        return carry

    lax.fori_loop(0, depth // 2, token_step, 0)

    parts = []
    for part in range(TEAMS):
        lines = slice(part * team_rows, (part + 1) * team_rows)
        mixed = acc_ref[lines, 0:team_width] * (1.0 / acc_ref[lines, team_width : team_width + 1])
        mixed = jnp.where(token_heads, mixed, 0.0)
        joined = mixed[0:tokens_dev]
        for head in range(1, team):
            joined = joined + mixed[head * tokens_dev : (head + 1) * tokens_dev]
        parts.append(joined.astype(BF16))
    token_mix = jnp.concatenate(parts, axis=1)
    updated = feat_ref[...] + mm(token_mix, tp_ref[3])
    to_atom_load.wait()
    rowsx_ref[2] = mm(updated.astype(BF16), to_atom_ref[...]).astype(BF16)
    row_sides.start()
    row_far.start()

    areas = ((0, PAD, 0), (PAD, PAD + atoms_dev, 1), (PAD + atoms_dev, 2 * PAD + atoms_dev, 2))

    def members(low, high, slot):
        shape = (high - low, 3 * tokens_dev)
        place = me * atoms_dev + low - PAD + lax.broadcasted_iota(jnp.int32, shape, 0)
        place = place.astype(F32)
        first, end = (
            jnp.concatenate([rngx_ref[slot + i, k : k + 1, 0:tokens_dev] for i in range(3)], axis=1).astype(F32)
            for k in range(2)
        )
        return jnp.where((place >= first) & (place < end), 1.0, 0.0).astype(BF16)

    x_ref[0:PAD] = encx_ref[0, atoms_dev - PAD : atoms_dev].astype(F32)
    x_ref[PAD + atoms_dev :] = encx_ref[2, 0:PAD].astype(F32)
    belongs = [members(*area) for area in areas]
    for sides in (mask_sides, range_sides, range_far, atom_sides, bias_sides, *enc_sides):
        sides.sent()
    if depth == 3:
        sent(z_copy, order(2))
    elif depth > 3:
        pl.when(inside)(lambda: sent(z_copy, order(2)))
    for step in range(depth):
        if step > 2:
            sent(z_copy, order(step))
        sent(y_copy, step)
        sent(c_copy, step, 0)
        sent(c_copy, step, 1)
    row_sides.receive()
    row_far.receive()
    for belong, (low, high, slot) in zip(belongs, areas):
        tall_rows = rowsx_ref[slot : slot + 3].reshape(3 * tokens_dev, channels)
        x_ref[low:high] = x_ref[low:high] + mm(belong, tall_rows)

    project(HALF, [(0, atoms_dev + 2 * PAD)])
    outside(HALF)
    whole(HALF, 0)
    whole(HALF + 1, 1)

    def keep_decoded(group, rows):
        for a, b in group:
            out_ref[0, a - PAD : b - PAD] = rows.astype(BF16)

    attend_all(HALF + 2, range(windows))
    transition(HALF + 2, [(PAD, PAD + atoms_dev)], keep_decoded)

    row_sides.sent()
    row_far.sent()


def shards(
    count,
    atoms,
    s_cond,
    token_start,
    token_len,
    atom_mask,
    atom_bias,
    pair_bias,
    atom_proj,
    atom_up,
    atom_down,
    atom_gains,
    to_token,
    token_proj,
    token_gain,
    to_atom,
):
    atoms_dev, channels = atoms.shape[1:]
    tokens_dev, width = s_cond.shape
    layers = 2 * HALF
    vmem = pl.BlockSpec(memory_space=pltpu.VMEM)
    hbm = pl.BlockSpec(memory_space=pl.ANY)
    depth = count // 4
    spread = atoms_dev + 2 * PAD
    return pl.pallas_call(
        functools.partial(kernel, count),
        out_shape=pltpu.VMEM(atoms.shape, BF16),
        in_specs=[hbm] * 15,
        out_specs=vmem,
        scratch_shapes=[
            pltpu.VMEM(token_start.shape, jnp.int32),
            pltpu.VMEM(token_len.shape, jnp.int32),
            pltpu.VMEM(atom_mask.shape, jnp.int32),
            pltpu.VMEM(atom_gains.shape, F32),
            pltpu.VMEM(token_gain.shape, F32),
            pltpu.VMEM((spread, channels), BF16),
            pltpu.VMEM((spread, channels), F32),
            pltpu.VMEM((2, 2, spread, channels), BF16),
            pltpu.VMEM((2, spread, channels), BF16),
            pltpu.VMEM((spread, channels), BF16),
            pltpu.VMEM((spread, channels), BF16),
            pltpu.VMEM((spread, 2 * atom_up.shape[3]), F32),
            pltpu.VMEM((spread, atom_up.shape[3]), BF16),
            pltpu.VMEM((HA, atoms_dev + 2 * EDGE, WK), F32),
            pltpu.VMEM((2, HA, EDGE - WQ + RIM % WQ, WK), BF16),
            pltpu.VMEM((2, HA, EDGE, WK), BF16),
            pltpu.VMEM(pair_bias.shape, BF16),
            pltpu.VMEM((layers, channels, 3 * channels), BF16),
            pltpu.VMEM((layers, channels, channels), BF16),
            pltpu.VMEM((layers, channels, 2 * atom_up.shape[3]), BF16),
            pltpu.VMEM(atom_down.shape, BF16),
            pltpu.VMEM(to_token.shape, BF16),
            pltpu.VMEM(to_atom.shape, BF16),
            pltpu.VMEM(s_cond.shape, BF16),
            pltpu.VMEM(token_proj.shape, BF16),
            pltpu.VMEM((3, atoms_dev // LANES, LANES), jnp.int32),
            pltpu.VMEM((atoms_dev // WQ + 2 * SPARE[0], HA * WQ, WK), BF16),
            pltpu.VMEM((5, 8, pl.cdiv(tokens_dev, LANES) * LANES), jnp.int32),
            pltpu.VMEM((3, atoms_dev, channels), BF16),
            pltpu.VMEM((5, tokens_dev, channels), BF16),
            pltpu.VMEM((count, tokens_dev, width), BF16),
            pltpu.VMEM((tokens_dev, width), F32),
            pltpu.VMEM((HT * tokens_dev, width), BF16),
            pltpu.VMEM((HT * tokens_dev, pl.cdiv(width // TEAMS + 1, LANES) * LANES), F32),
            pltpu.VMEM((HT * tokens_dev, LANES), F32),
            pltpu.SemaphoreType.DMA((19,)),
            pltpu.SemaphoreType.DMA((7, 2)),
            pltpu.SemaphoreType.DMA((7, 2)),
            pltpu.SemaphoreType.DMA((2, 2)),
            pltpu.SemaphoreType.DMA((2, 2)),
            pltpu.SemaphoreType.DMA((depth, U_PARTS)),
            pltpu.SemaphoreType.DMA((depth, U_PARTS)),
            pltpu.SemaphoreType.DMA((2, depth, U_PARTS)),
            pltpu.SemaphoreType.DMA((count, U_PARTS)),
        ],
        compiler_params=pltpu.CompilerParams(
            collective_id=0, has_side_effects=True, vmem_limit_bytes=60 * 1024 * 1024
        ),
    )(
        atoms,
        s_cond,
        token_start,
        token_len,
        atom_mask,
        atom_bias,
        pair_bias,
        atom_proj,
        atom_up,
        atom_down,
        atom_gains,
        to_token,
        token_proj,
        token_gain,
        to_atom,
    )


def solution(mesh):
    placed = (
        P("groups", "seq", None),
        P(("groups", "seq"), None),
        P(("groups", "seq")),
        P(("groups", "seq")),
        P(("groups", "seq")),
        P("groups", "seq", None),
        P("groups", "seq", None),
        P(),
        P(),
        P(),
        P(),
        P(),
        P(),
        P(),
        P(),
    )
    return jax.shard_map(
        functools.partial(shards, mesh.shape["seq"]),
        mesh=mesh,
        in_specs=placed,
        out_specs=P("groups", "seq", None),
        check_vma=False,
    )
```
